32 devices in a mesh: space: 16 (over z, y, core), grp: 2 (over x).
Axes of the slice: x: 2, y: 2, z: 4, core: 2. Of those that a mesh axis runs over, the one named last changes fastest.
Arguments:
- diag_blocks: float32 [16, 2, 128, 128], P('space', 'grp'), may hold values from -0.4 to 0.4
- x_coupling: float32 [16, 2, 128, 128], P('space', 'grp'), may hold values from -0.35 to 0.35
- y_coupling: float32 [16, 2, 128, 128], P('space', 'grp'), may hold values from -0.35 to 0.35
- levels: float32 [16, 2, 128], P('space', 'grp'), may hold values from -2 to 2
- listed: int32 [16, 2, 2], P('space', 'grp'), may hold values 0 or 1
Outputs:
- density_diag: float32 [16, 2, 128, 128], P('space', 'grp')
- density_x: float32 [16, 2, 128, 128], P('space', 'grp')
- density_y: float32 [16, 2, 128, 128], P('space', 'grp')
The draws below stay inside these ranges and needn't reach their ends.
Inputs may be any that keep to these rules, and one draw needn't show every extreme that they name: listed[i,j,0] keeps the coupling of block (i,j) with (i+1,j), listed[i,j,1] that with (i,j+1).
All inputs are finite; a program needn't handle non-finite values.
Results may differ from the reference program's by a relative error of at most 0.0037.
Values sent between devices are 32-bit elements; how exact they have to be, the bound alone decides.
A program may use at most 64 MiB of HBM per device.

```python
import jax
import jax.numpy as jnp
from jax import lax

BLK = 128
NX = 16
NY = 2


def set_ends(entries, stream_key, low, largest):
    dims = entries.shape
    place = [jax.random.randint(jax.random.fold_in(stream_key, axis), (), 0, dims[axis]) for axis in range(len(dims))]
    entries = entries.at[tuple(place)].set(low)
    longest = dims.index(max(dims))
    place[longest] = (place[longest] + 1) % dims[longest]
    return entries.at[tuple(place)].set(largest)


def steps_of(stream_key, shape, shards, low, top_value):
    factor_of, own = 1.0, jax.random.fold_in(stream_key, 6)
    for position, shards_of in shards:
        draws = jnp.exp(jax.random.uniform(jax.random.fold_in(own, position), (shards_of,), jnp.float32, low / len(shards), top_value / len(shards)))
        factor_of = factor_of * jnp.repeat(draws, shape[position] // shards_of).reshape([-1 if axis == position else 1 for axis in range(len(shape))])
    return factor_of


def normal_values(own_key, dims, deviation, limit, shards=(), kind=jnp.bfloat16):
    loudness = steps_of(own_key, dims, shards, -0.22, 0.18) if shards else 1.0
    values = jax.random.normal(own_key, dims, jnp.float32) * deviation * loudness
    return jnp.minimum(jnp.maximum(values, -limit), limit).astype(kind)


def setup_inputs(seed: int = 0) -> dict:
    seeds = jax.random.split(jax.random.key(seed), 6)
    diag_blocks = normal_values(seeds[0], (NX, NY, BLK, BLK), 0.06, 0.4, ((0, 16), (1, 2)), jnp.float32)
    x_coupling = normal_values(seeds[1], (NX, NY, BLK, BLK), 0.05, 0.35, ((0, 16), (1, 2)), jnp.float32)
    y_coupling = normal_values(seeds[2], (NX, NY, BLK, BLK), 0.05, 0.35, ((0, 16), (1, 2)), jnp.float32)
    levels = jnp.clip(jax.random.uniform(seeds[3], (NX, NY, BLK), jnp.float32, -2.0, 2.0) * steps_of(seeds[3], (NX, NY, BLK), ((0, 16), (1, 2)), -0.4, 0.0), -2.0, 2.0)
    listed = set_ends((jax.random.randint(seeds[4], (NX, NY, 2), 0, 4) < 3).astype(jnp.int32), jax.random.fold_in(seeds[4], 1), 0, 1)
    return {"diag_blocks": diag_blocks, "x_coupling": x_coupling, "y_coupling": y_coupling, "levels": levels, "listed": listed}


hubbard = 1.0

def symmetric(matrix):
    return 0.5 * (matrix + matrix.T)

def assemble(center, nbr_diag, nbr_coup):
    block_width = center.shape[0]
    zero_block = jnp.zeros((block_width, block_width), center.dtype)
    top_row = jnp.concatenate([center] + [nbr_coup[member].T for member in range(4)], axis=1)
    row_list = [top_row]
    for member in range(4):
        pieces = [nbr_coup[member]] + [nbr_diag[member] if column_slot == member else zero_block for column_slot in range(4)]
        row_list.append(jnp.concatenate(pieces, axis=1))
    return jnp.concatenate(row_list, axis=0)

def density_column(matrix):
    order_size = matrix.shape[0]
    block_width = order_size // 5
    matrix_half = matrix.astype(jnp.bfloat16)
    square = jnp.dot(matrix_half, matrix_half, preferred_element_type=jnp.float32)
    square_half = square.astype(jnp.bfloat16)
    fourth = jnp.dot(square_half, square_half, preferred_element_type=jnp.float32)
    scale_four = jnp.sqrt(jnp.sum(fourth * fourth) + 1e-06)
    scale_two = jnp.sqrt(scale_four)
    scale_one = jnp.sqrt(scale_two)
    identity = jnp.eye(order_size, dtype=jnp.float32)
    initial = (matrix / scale_one).astype(jnp.bfloat16)
    factor = (3.0 * identity - square / scale_two).astype(jnp.bfloat16)
    iterate = (0.5 * jnp.dot(initial, factor, preferred_element_type=jnp.float32)).astype(jnp.bfloat16)
    column = iterate[:, :block_width]
    applied_once = jnp.dot(iterate, column, preferred_element_type=jnp.float32).astype(jnp.bfloat16)
    applied_twice = jnp.dot(iterate, applied_once, preferred_element_type=jnp.float32)
    sign_part = 0.5 * (3.0 * column.astype(jnp.float32) - applied_twice)
    density = 0.5 * (identity[:, :block_width] - sign_part)
    return density.reshape(5, block_width, block_width)

def sweep(diag_all, x_all, y_all):
    size_x = diag_all.shape[0]
    size_y = diag_all.shape[1]
    block_width = diag_all.shape[2]
    widths = ((1, 1), (1, 1), (0, 0), (0, 0))
    pad_diag = jnp.pad(diag_all, widths)
    pad_x = jnp.pad(x_all, widths)
    pad_y = jnp.pad(y_all, widths)
    zero_index = jnp.int32(0)

    def one_site(flat):
        row_index = flat // size_y
        col_index = flat % size_y

        def pick(array, shift_x, shift_y):
            start_x = (row_index + (1 + shift_x)).astype(jnp.int32)
            start_y = (col_index + (1 + shift_y)).astype(jnp.int32)
            return lax.dynamic_slice(array, (start_x, start_y, zero_index, zero_index), (1, 1, block_width, block_width))[0, 0]
        center = pick(pad_diag, 0, 0)
        nbr_diag = jnp.stack([pick(pad_diag, -1, 0), pick(pad_diag, 1, 0), pick(pad_diag, 0, -1), pick(pad_diag, 0, 1)])
        nbr_coup = jnp.stack([pick(pad_x, -1, 0), pick(pad_x, 0, 0).T, pick(pad_y, 0, -1), pick(pad_y, 0, 0).T])
        return density_column(assemble(center, nbr_diag, nbr_coup))
    columns = lax.map(one_site, jnp.arange(size_x * size_y, dtype=jnp.int32))
    columns = columns.reshape(size_x, size_y, 5, block_width, block_width)
    diag_density = 0.5 * (columns[:, :, 0] + jnp.swapaxes(columns[:, :, 0], -1, -2))
    from_x = jnp.concatenate([columns[1:, :, 1], jnp.zeros_like(columns[:1, :, 1])], axis=0)
    x_density = 0.5 * (jnp.swapaxes(columns[:, :, 2], -1, -2) + from_x)
    from_y = jnp.concatenate([columns[:, 1:, 3], jnp.zeros_like(columns[:, :1, 3])], axis=1)
    y_density = 0.5 * (jnp.swapaxes(columns[:, :, 4], -1, -2) + from_y)
    return (diag_density, x_density, y_density)

def reference(diag_blocks, x_coupling, y_coupling, levels, listed):
    identity = jnp.eye(BLK, dtype=jnp.float32)
    pos_x = jnp.arange(NX, dtype=jnp.int32)[:, None]
    pos_y = jnp.arange(NY, dtype=jnp.int32)[None, :]
    flag_x = listed[:, :, 0].astype(jnp.float32) * (pos_x < NX - 1).astype(jnp.float32)
    flag_y = listed[:, :, 1].astype(jnp.float32) * (pos_y < NY - 1).astype(jnp.float32)
    onsite = 0.5 * (diag_blocks + jnp.swapaxes(diag_blocks, -1, -2)) + levels[..., None] * identity
    coup_x = x_coupling * flag_x[:, :, None, None]
    coup_y = y_coupling * flag_y[:, :, None, None]
    diag_one, x_one, y_one = sweep(onsite, coup_x, coup_y)
    onsite_two = onsite + hubbard * (diag_one - 0.5 * identity)
    coup_x_two = coup_x + hubbard * x_one
    coup_y_two = coup_y + hubbard * y_one
    diag_two, x_two, y_two = sweep(onsite_two, coup_x_two, coup_y_two)
    return (diag_two, x_two, y_two)
```

```python
import functools

import jax
import jax.numpy as jnp
from jax import lax
from jax.experimental import pallas as pl
from jax.experimental.pallas import tpu as pltpu
from jax.sharding import PartitionSpec as P

hubbard = 1.0
MESH = pl.DeviceIdType.MESH
F32 = jnp.float32
BF16 = jnp.bfloat16
K1, K3, K5, K7, K9 = -1.125, 1.21875, -0.84375, 0.28125, -0.03125


def mm(a, b):
    return jnp.dot(a, b, preferred_element_type=F32)


def iotas(shape):
    return lax.broadcasted_iota(jnp.int32, shape, 0), lax.broadcasted_iota(jnp.int32, shape, 1)


def eye(w):
    i, l = iotas((w, w))
    return i == l


def pack(m):
    w = m.shape[0]
    h = w // 2
    i, l = iotas((h, w))
    d = l - i
    top, low = m[:h], m[h:]
    rows = jnp.where((d >= 0) & (d < h), top, low)
    rows = jnp.where((d == 0) | (d == h), 0.5 * rows, rows)
    across = jnp.sum(jnp.where(d == h, top, 0.0), axis=0, keepdims=True)
    return rows, jnp.broadcast_to(across, (8, w))


def unpack(p):
    w = p.shape[1]
    h = w // 2
    i, l = iotas((h, w))
    d = l - i
    inside = (d >= 0) & (d < h)
    rows = p[:h]
    across = jnp.broadcast_to(p[h : h + 1], (h, w))
    top = jnp.where(inside, rows, jnp.where(d == h, across, 0.0))
    low = jnp.where(inside, 0.0, rows)
    half = jnp.concatenate([top, low], axis=0)
    return half + half.T


def density_columns(nb, w, am, v1f, sx, fb, v3f, v5f, vb):
    n = nb * w

    def bl(i):
        return slice(i * w, (i + 1) * w)

    tiles = [slice(i * w, min(i + 2, nb) * w) for i in range(0, nb, 2)]
    for tile in tiles:
        sx[:, tile] = mm(am[...], am[:, tile]).astype(BF16)
    squares = jnp.zeros((8, w), F32)

    def add_squares(f):
        return jnp.sum((f * f).reshape(n // 8, 8, w), axis=0)

    r = mm(sx[...], jnp.concatenate([sx[:, bl(0)], am[:, bl(0)]], axis=1))
    fb[:, bl(0)] = r[:, :w].astype(BF16)
    squares = squares + add_squares(r[:, :w])
    v3f[...] = r[:, w:]
    vb[:, :w] = r[:, w:].astype(BF16)
    last = nb - 1
    for i in range(1, last, 2):
        pair = [i] if i == last else [i, i + 1]
        r = mm(sx[...], sx[:, i * w : (i + len(pair)) * w])
        for at, j in enumerate(pair):
            f = r[:, bl(at)]
            fb[:, bl(j)] = f.astype(BF16)
            squares = squares + add_squares(f)
    if nb % 2 == 0:
        r = mm(sx[...], jnp.concatenate([sx[:, bl(last)], vb[:, :w]], axis=1))
        fb[:, bl(last)] = r[:, :w].astype(BF16)
        squares = squares + add_squares(r[:, :w])
        v5 = r[:, w:]
    else:
        v5 = mm(sx[...], vb[:, :w])
    v5f[...] = v5
    vb[:, w:] = v5.astype(BF16)
    v79 = mm(fb[...], vb[...])
    total = jnp.sum(jnp.sum(squares, axis=1, keepdims=True), axis=0, keepdims=True)
    inverse = lax.rsqrt(lax.rsqrt(lax.rsqrt(total + 1e-06)))
    return v79, inverse


def combine(v1, v3, v5, v7, v9, inverse):
    square = inverse * inverse
    inner = K7 * v7 + square * (K9 * v9)
    inner = K5 * v5 + square * inner
    inner = K3 * v3 + square * inner
    return inverse * (K1 * v1 + square * inner)


def kernel(
    sizes, diag_hbm, x_hbm, y_hbm, lev_hbm, list_hbm, out_ref,
    din, xin, yin, lin, fin, in_sems,
    coup_out, diag_out, diag_out2, rd1, rb1, rd2, rc2, rf3,
    am, v1f, sx, fb, v3f, v5f, vb, cols, rowf,
    send_sems, recv_sems,
):
    nx, ny = sizes
    w = din.shape[0]
    merged = ny == 2
    slot = (1, 2, 3, 3) if merged else (1, 2, 3, 4)
    nb = slot[3] + 1
    h = w // 2
    ix = lax.axis_index("space")
    iy = lax.axis_index("grp")
    even = lax.rem(ix, 2) == 0
    has = [ix > 0, ix < nx - 1, iy > 0, iy < ny - 1]
    dev = [
        (jnp.maximum(ix - 1, 0), iy),
        (jnp.minimum(ix + 1, nx - 1), iy),
        (ix, jnp.maximum(iy - 1, 0)),
        (ix, jnp.minimum(iy + 1, ny - 1)),
    ]

    def bl(i):
        return slice(i * w, (i + 1) * w)

    barrier = pltpu.get_barrier_semaphore()
    for k in range(4):
        @pl.when(has[k])
        def _():
            pl.semaphore_signal(barrier, inc=1, device_id=dev[k], device_id_type=MESH)

    loads = [
        pltpu.make_async_copy(diag_hbm.at[0, 0], din, in_sems.at[0]),
        pltpu.make_async_copy(x_hbm.at[0, 0], xin, in_sems.at[1]),
        pltpu.make_async_copy(y_hbm.at[0, 0], yin, in_sems.at[2]),
        pltpu.make_async_copy(lev_hbm.at[0], lin, in_sems.at[3]),
        pltpu.make_async_copy(list_hbm.at[0], fin, in_sems.at[4]),
    ]
    for load in loads:
        load.start()
    for k in range(2 if merged else 4):
        @pl.when(jnp.logical_not(has[k]))
        def _():
            rd1[slot[k] - 1] = jnp.zeros((h + 8, w), F32)
            rd2[slot[k] - 1] = jnp.zeros((h + 8, w), F32)
            rc2[slot[k] - 1] = jnp.zeros((w, w), F32)
            if k % 2 == 0:
                rb1[k // 2] = jnp.zeros((w, w), F32)
    for k in (1, 3):
        @pl.when(jnp.logical_not(has[k]))
        def _():
            rf3[k // 2] = jnp.zeros((w, w), F32)
    for i in range(1, nb):
        for j in range(1, nb):
            if i != j:
                am[bl(i), bl(j)] = jnp.zeros((w, w), BF16)
    for load in loads:
        load.wait()
    one_eye = eye(w)
    flag_x = fin[0, 0].astype(F32) * (ix < nx - 1).astype(F32)
    flag_y = fin[0, 1].astype(F32) * (iy < ny - 1).astype(F32)
    raw = din[...]
    onsite = 0.5 * (raw + raw.T) + jnp.where(one_eye, jnp.broadcast_to(lin[...], (w, w)), 0.0)
    diag_out[:h], diag_out[h:] = pack(onsite)
    coup_out[0] = xin[...] * flag_x
    coup_out[1] = yin[...] * flag_y

    count = sum(here.astype(jnp.int32) for here in has)
    pl.semaphore_wait(barrier, count)

    def transfer(src, dst, index_send, index_recv, k):
        return pltpu.make_async_remote_copy(
            src_ref=src, dst_ref=dst, send_sem=send_sems.at[index_send],
            recv_sem=recv_sems.at[index_recv], device_id=dev[k], device_id_type=MESH,
        )

    def diag1(k):
        return transfer(diag_out, rd1.at[slot[k ^ 1] - 1], k, k ^ 1, k)

    def coup1(k):
        return transfer(coup_out.at[k // 2], rb1.at[k // 2], 4 + k // 2, 4 + k // 2, k)

    def diag2(k):
        return transfer(diag_out2, rd2.at[slot[k ^ 1] - 1], 6 + k, 6 + (k ^ 1), k)

    def coup2(k):
        return transfer(cols.at[0, bl(slot[k]), :], rc2.at[slot[k ^ 1] - 1], 10 + k, 10 + (k ^ 1), k)

    def coup3(k):
        return transfer(cols.at[1, bl(slot[k]), :], rf3.at[k // 2], 14 + k // 2, 14 + k // 2, k)

    def start(copies, first=None):
        for make, k in copies:
            there = has[k]
            if first is not None:
                there = there & (even if first else jnp.logical_not(even))

            @pl.when(there)
            def _():
                make(k).start()

    ys = [(coup1, 3), (diag1, 3), (diag1, 2)]
    start(ys, True)
    start([(coup1, 1), (diag1, 1), (diag1, 0)])
    start(ys, False)

    am[bl(0), bl(0)] = onsite.astype(BF16)
    v1f[bl(0), :] = onsite

    def own_coupling(axis):
        s = slot[2 * axis + 1]
        coup = coup_out[axis]
        coup_t = coup.T
        am[bl(0), bl(s)] = coup.astype(BF16)
        am[bl(s), bl(0)] = coup_t.astype(BF16)
        v1f[bl(s), :] = coup_t

    def other_coupling(axis):
        s = slot[2 * axis]
        coup = rb1[axis]
        am[bl(0), bl(s)] = coup.T.astype(BF16)
        am[bl(s), bl(0)] = coup.astype(BF16)
        v1f[bl(s), :] = coup

    own_coupling(0)
    if merged:
        pl.when(has[3])(lambda: own_coupling(1))
    else:
        own_coupling(1)

    def wait_recv(copies):
        for make, k in copies:
            @pl.when(has[k])
            def _():
                make(k ^ 1).wait_recv()

    wait_recv([(coup1, 0), (diag1, 0), (diag1, 1)])
    other_coupling(0)
    for s in (1, 2):
        am[bl(s), bl(s)] = unpack(rd1[s - 1]).astype(BF16)
    wait_recv([(coup1, 2), (diag1, 2), (diag1, 3)])
    if merged:
        pl.when(has[2])(lambda: other_coupling(1))
    else:
        other_coupling(1)
    for s in range(3, nb):
        am[bl(s), bl(s)] = unpack(rd1[s - 1]).astype(BF16)

    v79, inverse = density_columns(nb, w, am, v1f, sx, fb, v3f, v5f, vb)

    def finish(step, s):
        r = bl(s)
        cols[step, r, :] = combine(v1f[r, :], v3f[r, :], v5f[r, :], v79[r, :w], v79[r, w:], inverse)

    for s in range(3, nb):
        finish(0, s)
    ys = [(coup2, 3), (coup2, 2)]
    start(ys, True)
    finish(0, 1)
    finish(0, 2)
    start([(coup2, 1), (coup2, 0)])
    finish(0, 0)
    c0 = cols[0, bl(0), :]
    two = v1f[bl(0), :] + (0.5 * hubbard) * (c0 + c0.T)
    diag_out2[:h], diag_out2[h:] = pack(two)
    start([(diag2, 3), (diag2, 2)], True)
    start([(diag2, 1), (diag2, 0)])
    start(ys + [(diag2, 3), (diag2, 2)], False)

    am[bl(0), bl(0)] = two.astype(BF16)
    v1f[bl(0), :] = two
    for s in range(1, nb):
        rowf[s - 1] = (v1f[bl(s), :] + (0.5 * hubbard) * cols[0, bl(s), :]).T

    def arrived2(s):
        row = rowf[s - 1] + (0.5 * hubbard) * rc2[s - 1]
        col = row.T
        am[bl(0), bl(s)] = row.astype(BF16)
        am[bl(s), bl(0)] = col.astype(BF16)
        v1f[bl(s), :] = col
        am[bl(s), bl(s)] = unpack(rd2[s - 1]).astype(BF16)

    wait_recv([(coup2, 0), (coup2, 1), (diag2, 0), (diag2, 1)])
    for s in (1, 2):
        arrived2(s)
    wait_recv([(coup2, 2), (coup2, 3), (diag2, 2), (diag2, 3)])
    for s in range(3, nb):
        arrived2(s)

    v79, inverse = density_columns(nb, w, am, v1f, sx, fb, v3f, v5f, vb)

    for s in range(3, nb):
        finish(1, s)
    start([(coup3, 2)])
    finish(1, 1)
    start([(coup3, 0)])
    finish(1, 2)
    finish(1, 0)
    c0 = cols[1, bl(0), :]
    out_ref[0] = 0.5 * (c0 + c0.T) + jnp.where(one_eye, 0.5, 0.0)
    half_x = 0.5 * cols[1, bl(2), :].T
    half_y = jnp.where(has[3], 0.5 * cols[1, bl(slot[3]), :].T, 0.0)
    wait_recv([(coup3, 1)])
    out_ref[1] = half_x + 0.5 * rf3[0]
    wait_recv([(coup3, 3)])
    out_ref[2] = half_y + 0.5 * rf3[1]
    for k in range(4):
        @pl.when(has[k])
        def _():
            if k % 2:
                coup1(k).wait_send()
            else:
                coup3(k).wait_send()
            diag1(k).wait_send()
            coup2(k).wait_send()
            diag2(k).wait_send()


def write_out(in_ref, od_ref, ox_ref, oy_ref, sems):
    copies = [
        pltpu.make_async_copy(in_ref.at[i], ref.at[0, 0], sems.at[i])
        for i, ref in enumerate((od_ref, ox_ref, oy_ref))
    ]
    for copy in copies:
        copy.start()
    for copy in copies:
        copy.wait()


def per_device(diag_blocks, x_coupling, y_coupling, levels, listed):
    w = diag_blocks.shape[-1]
    sizes = (lax.axis_size("space"), lax.axis_size("grp"))
    nb = 4 if sizes[1] == 2 else 5
    n = nb * w
    half = w // 2 + 8
    block = jax.ShapeDtypeStruct((1, 1, w, w), F32)
    any_spec = pl.BlockSpec(memory_space=pl.ANY)
    vmem_spec = pl.BlockSpec(memory_space=pltpu.VMEM)
    results = pl.pallas_call(
        functools.partial(kernel, sizes),
        out_shape=pltpu.VMEM((3, w, w), F32),
        in_specs=[any_spec] * 5,
        out_specs=vmem_spec,
        scratch_shapes=[
            pltpu.VMEM((w, w), F32),
            pltpu.VMEM((w, w), F32),
            pltpu.VMEM((w, w), F32),
            pltpu.VMEM((1, w), F32),
            pltpu.SMEM((1, 2), jnp.int32),
            pltpu.SemaphoreType.DMA((5,)),
            pltpu.VMEM((2, w, w), F32),
            pltpu.VMEM((half, w), F32),
            pltpu.VMEM((half, w), F32),
            pltpu.VMEM((nb - 1, half, w), F32),
            pltpu.VMEM((2, w, w), F32),
            pltpu.VMEM((nb - 1, half, w), F32),
            pltpu.VMEM((nb - 1, w, w), F32),
            pltpu.VMEM((2, w, w), F32),
            pltpu.VMEM((n, n), BF16),
            pltpu.VMEM((n, w), F32),
            pltpu.VMEM((n, n), BF16),
            pltpu.VMEM((n, n), BF16),
            pltpu.VMEM((n, w), F32),
            pltpu.VMEM((n, w), F32),
            pltpu.VMEM((n, 2 * w), BF16),
            pltpu.VMEM((2, n, w), F32),
            pltpu.VMEM((nb - 1, w, w), F32),
            pltpu.SemaphoreType.DMA((16,)),
            pltpu.SemaphoreType.DMA((16,)),
        ],
        compiler_params=pltpu.CompilerParams(collective_id=0, has_side_effects=True),
    )(diag_blocks, x_coupling, y_coupling, levels, listed)
    return pl.pallas_call(
        write_out,
        out_shape=(block, block, block),
        in_specs=[vmem_spec],
        out_specs=(any_spec,) * 3,
        scratch_shapes=[pltpu.SemaphoreType.DMA((3,))],
    )(pltpu.with_memory_space_constraint(results, pltpu.VMEM))


def solution(mesh):
    blocks = P("space", "grp", None, None)
    rows = P("space", "grp", None)
    return jax.shard_map(
        per_device,
        mesh=mesh,
        in_specs=(blocks, blocks, blocks, rows, rows),
        out_specs=(blocks, blocks, blocks),
        check_vma=False,
    )
```

```python
import functools

import jax
import jax.numpy as jnp
from jax import lax
from jax.experimental import pallas as pl
from jax.experimental.pallas import tpu as pltpu
from jax.sharding import PartitionSpec as P

hubbard = 1.0
MESH = pl.DeviceIdType.MESH
F32 = jnp.float32
BF16 = jnp.bfloat16
K1, K3, K5, K7, K9 = -1.125, 1.21875, -0.84375, 0.28125, -0.03125


def mm(a, b):
    return jnp.dot(a, b, preferred_element_type=F32)


def iotas(shape):
    return lax.broadcasted_iota(jnp.int32, shape, 0), lax.broadcasted_iota(jnp.int32, shape, 1)


def eye(w):
    i, l = iotas((w, w))
    return i == l


def pack(m):
    w = m.shape[0]
    h = w // 2
    i, l = iotas((h, w))
    d = l - i
    top, low = m[:h], m[h:]
    rows = jnp.where((d >= 0) & (d < h), top, low)
    rows = jnp.where((d == 0) | (d == h), 0.5 * rows, rows)
    across = jnp.sum(jnp.where(d == h, top, 0.0), axis=0, keepdims=True)
    return rows, jnp.broadcast_to(across, (8, w))


def unpack(p):
    w = p.shape[1]
    h = w // 2
    i, l = iotas((h, w))
    d = l - i
    inside = (d >= 0) & (d < h)
    rows = p[:h]
    across = jnp.broadcast_to(p[h : h + 1], (h, w))
    top = jnp.where(inside, rows, jnp.where(d == h, across, 0.0))
    low = jnp.where(inside, 0.0, rows)
    half = jnp.concatenate([top, low], axis=0)
    return half + half.T


def square(nb, w, am, sx):
    for i in range(0, nb, 2):
        tile = slice(i * w, min(i + 2, nb) * w)
        sx[:, tile] = mm(am[...], am[:, tile]).astype(BF16)


def powers(nb, w, am, sx, fb, v3f, v5f, vb):
    n = nb * w
    at = nb // 2 * w
    halves = (slice(0, at), slice(at, n))

    def bl(i):
        return slice(i * w, (i + 1) * w)

    squares = [jnp.zeros((8, w), F32)]

    def keep_fourth(rows, j, f):
        fb[rows, bl(j)] = f.astype(BF16)
        squares[0] = squares[0] + jnp.sum((f * f).reshape(-1, 8, w), axis=0)

    right = jnp.concatenate([sx[:, bl(0)], am[:, bl(0)]], axis=1)
    for rows in halves:
        r = mm(sx[rows, :], right)
        keep_fourth(rows, 0, r[:, :w])
        v3f[rows, :] = r[:, w:]
        vb[rows, :w] = r[:, w:].astype(BF16)
    last = nb - 1
    for i in range(1, last, 2):
        pair = [i] if i == last else [i, i + 1]
        right = sx[:, i * w : (i + len(pair)) * w]
        for rows in halves:
            r = mm(sx[rows, :], right)
            for at, j in enumerate(pair):
                keep_fourth(rows, j, r[:, bl(at)])
    right = vb[:, :w]
    if nb % 2 == 0:
        right = jnp.concatenate([sx[:, bl(last)], right], axis=1)
    for rows in halves:
        r = mm(sx[rows, :], right)
        if nb % 2 == 0:
            keep_fourth(rows, last, r[:, :w])
        v5 = r[:, -w:]
        v5f[rows, :] = v5
        vb[rows, w:] = v5.astype(BF16)
    return jnp.sum(jnp.sum(squares[0], axis=1, keepdims=True), axis=0, keepdims=True)


def coefficients(total):
    r = lax.rsqrt(lax.rsqrt(lax.rsqrt(total + 1e-06)))
    r2 = r * r
    r3 = r2 * r
    r4 = r2 * r2
    return K1 * r, K3 * r3, K5 * (r4 * r), K7 * (r4 * r3), K9 * (r4 * r4 * r)


def kernel(
    sizes, diag_hbm, x_hbm, y_hbm, lev_hbm, list_hbm, out_ref,
    din, xin, yin, lin, fin, in_sems,
    coup_out, diag_out, diag_out2, rd1, rb1, rd2, rc2, rf3,
    am, v1f, sx, fb, v3f, v5f, vb, cols, rowf,
    send_sems, recv_sems,
):
    nx, ny = sizes
    w = din.shape[0]
    merged = ny == 2
    slot = (1, 2, 3, 3) if merged else (1, 2, 3, 4)
    nb = slot[3] + 1
    h = w // 2
    ix = lax.axis_index("space")
    iy = lax.axis_index("grp")
    even = lax.rem(ix, 2) == 0
    has = [ix > 0, ix < nx - 1, iy > 0, iy < ny - 1]
    dev = [
        (jnp.maximum(ix - 1, 0), iy),
        (jnp.minimum(ix + 1, nx - 1), iy),
        (ix, jnp.maximum(iy - 1, 0)),
        (ix, jnp.minimum(iy + 1, ny - 1)),
    ]

    def bl(i):
        return slice(i * w, (i + 1) * w)

    barrier = pltpu.get_barrier_semaphore()
    for k in range(4):
        @pl.when(has[k])
        def _():
            pl.semaphore_signal(barrier, inc=1, device_id=dev[k], device_id_type=MESH)

    loads = [
        pltpu.make_async_copy(diag_hbm.at[0, 0], din, in_sems.at[0]),
        pltpu.make_async_copy(x_hbm.at[0, 0], xin, in_sems.at[1]),
        pltpu.make_async_copy(y_hbm.at[0, 0], yin, in_sems.at[2]),
        pltpu.make_async_copy(lev_hbm.at[0], lin, in_sems.at[3]),
        pltpu.make_async_copy(list_hbm.at[0], fin, in_sems.at[4]),
    ]
    for load in loads:
        load.start()
    for k in range(2 if merged else 4):
        @pl.when(jnp.logical_not(has[k]))
        def _():
            rd1[slot[k] - 1] = jnp.zeros((h + 8, w), F32)
            rd2[slot[k] - 1] = jnp.zeros((h + 8, w), F32)
            rc2[slot[k] - 1] = jnp.zeros((w, w), F32)
            if k % 2 == 0:
                rb1[k // 2] = jnp.zeros((w, w), F32)
    for k in (1, 3):
        @pl.when(jnp.logical_not(has[k]))
        def _():
            rf3[k // 2] = jnp.zeros((w, w), F32)
    for i in range(1, nb):
        for j in range(1, nb):
            if i != j:
                am[bl(i), bl(j)] = jnp.zeros((w, w), BF16)
    for load in loads:
        load.wait()
    one_eye = eye(w)
    flag_x = fin[0, 0].astype(F32) * (ix < nx - 1).astype(F32)
    flag_y = fin[0, 1].astype(F32) * (iy < ny - 1).astype(F32)
    raw = din[...]
    onsite = 0.5 * (raw + raw.T) + jnp.where(one_eye, jnp.broadcast_to(lin[...], (w, w)), 0.0)
    diag_out[:h], diag_out[h:] = pack(onsite)
    coup_out[0] = xin[...] * flag_x
    coup_out[1] = yin[...] * flag_y

    count = sum(here.astype(jnp.int32) for here in has)
    pl.semaphore_wait(barrier, count)

    def transfer(src, dst, index_send, index_recv, k):
        return pltpu.make_async_remote_copy(
            src_ref=src, dst_ref=dst, send_sem=send_sems.at[index_send],
            recv_sem=recv_sems.at[index_recv], device_id=dev[k], device_id_type=MESH,
        )

    def diag1(k):
        return transfer(diag_out, rd1.at[slot[k ^ 1] - 1], k, k ^ 1, k)

    def coup1(k):
        return transfer(coup_out.at[k // 2], rb1.at[k // 2], 4 + k // 2, 4 + k // 2, k)

    def diag2(k):
        return transfer(diag_out2, rd2.at[slot[k ^ 1] - 1], 6 + k, 6 + (k ^ 1), k)

    def coup2(k):
        return transfer(cols.at[0, bl(slot[k]), :], rc2.at[slot[k ^ 1] - 1], 10 + k, 10 + (k ^ 1), k)

    def coup3(k):
        return transfer(cols.at[1, bl(slot[k]), :], rf3.at[k // 2], 14 + k // 2, 14 + k // 2, k)

    def start(copies, first=None):
        for make, k in copies:
            there = has[k]
            if first is not None:
                there = there & (even if first else jnp.logical_not(even))

            @pl.when(there)
            def _():
                make(k).start()

    ys = [(coup1, 3), (diag1, 3), (diag1, 2)]
    start(ys)
    start([(coup1, 1), (diag1, 1), (diag1, 0)])

    am[bl(0), bl(0)] = onsite.astype(BF16)
    v1f[bl(0), :] = onsite

    def own_coupling(axis):
        s = slot[2 * axis + 1]
        coup = coup_out[axis]
        coup_t = coup.T
        am[bl(0), bl(s)] = coup.astype(BF16)
        am[bl(s), bl(0)] = coup_t.astype(BF16)
        v1f[bl(s), :] = coup_t

    def other_coupling(axis):
        s = slot[2 * axis]
        coup = rb1[axis]
        am[bl(0), bl(s)] = coup.T.astype(BF16)
        am[bl(s), bl(0)] = coup.astype(BF16)
        v1f[bl(s), :] = coup

    own_coupling(0)
    if merged:
        pl.when(has[3])(lambda: own_coupling(1))
    else:
        own_coupling(1)

    def wait_recv(copies):
        for make, k in copies:
            @pl.when(has[k])
            def _():
                make(k ^ 1).wait_recv()

    wait_recv([(coup1, 0), (diag1, 0), (diag1, 1)])
    other_coupling(0)
    for s in (1, 2):
        am[bl(s), bl(s)] = unpack(rd1[s - 1]).astype(BF16)
    wait_recv([(coup1, 2), (diag1, 2), (diag1, 3)])
    if merged:
        pl.when(has[2])(lambda: other_coupling(1))
    else:
        other_coupling(1)
    for s in range(3, nb):
        am[bl(s), bl(s)] = unpack(rd1[s - 1]).astype(BF16)

    square(nb, w, am, sx)
    total = powers(nb, w, am, sx, fb, v3f, v5f, vb)
    c1, c3, c5, c7, c9 = coefficients(total)

    def finish(step, s):
        parts = (slice(s * w, s * w + h), slice(s * w + h, (s + 1) * w))
        for r in parts:
            v79 = mm(fb[r, :], vb[...])
            low = c1 * v1f[r, :] + c3 * v3f[r, :] + c5 * v5f[r, :]
            cols[step, r, :] = low + c7 * v79[:, :w] + c9 * v79[:, w:]

    for s in range(3, nb):
        finish(0, s)
    ys = [(coup2, 3), (coup2, 2)]
    start(ys)
    finish(0, 1)
    finish(0, 2)
    start([(coup2, 1), (coup2, 0)])
    finish(0, 0)
    c0 = cols[0, bl(0), :]
    two = v1f[bl(0), :] + (0.5 * hubbard) * (c0 + c0.T)
    diag_out2[:h], diag_out2[h:] = pack(two)
    start([(diag2, 3), (diag2, 2)])
    start([(diag2, 1), (diag2, 0)])

    am[bl(0), bl(0)] = two.astype(BF16)
    v1f[bl(0), :] = two
    for s in range(1, nb):
        rowf[s - 1] = (v1f[bl(s), :] + (0.5 * hubbard) * cols[0, bl(s), :]).T

    def arrived2(s):
        row = rowf[s - 1] + (0.5 * hubbard) * rc2[s - 1]
        col = row.T
        am[bl(0), bl(s)] = row.astype(BF16)
        am[bl(s), bl(0)] = col.astype(BF16)
        v1f[bl(s), :] = col
        am[bl(s), bl(s)] = unpack(rd2[s - 1]).astype(BF16)

    wait_recv([(coup2, 0), (coup2, 1), (diag2, 0), (diag2, 1)])
    for s in (1, 2):
        arrived2(s)
    wait_recv([(coup2, 2), (coup2, 3), (diag2, 2), (diag2, 3)])
    for s in range(3, nb):
        arrived2(s)

    square(nb, w, am, sx)
    total = powers(nb, w, am, sx, fb, v3f, v5f, vb)
    c1, c3, c5, c7, c9 = coefficients(total)

    for s in range(3, nb):
        finish(1, s)
    start([(coup3, 2)])
    finish(1, 1)
    start([(coup3, 0)])
    finish(1, 2)
    finish(1, 0)
    c0 = cols[1, bl(0), :]
    out_ref[0] = 0.5 * (c0 + c0.T) + jnp.where(one_eye, 0.5, 0.0)
    half_x = 0.5 * cols[1, bl(2), :].T
    half_y = jnp.where(has[3], 0.5 * cols[1, bl(slot[3]), :].T, 0.0)
    wait_recv([(coup3, 1)])
    out_ref[1] = half_x + 0.5 * rf3[0]
    wait_recv([(coup3, 3)])
    out_ref[2] = half_y + 0.5 * rf3[1]
    for k in range(4):
        @pl.when(has[k])
        def _():
            if k % 2:
                coup1(k).wait_send()
            else:
                coup3(k).wait_send()
            diag1(k).wait_send()
            coup2(k).wait_send()
            diag2(k).wait_send()


def write_out(in_ref, od_ref, ox_ref, oy_ref, sems):
    copies = [
        pltpu.make_async_copy(in_ref.at[i], ref.at[0, 0], sems.at[i])
        for i, ref in enumerate((od_ref, ox_ref, oy_ref))
    ]
    for copy in copies:
        copy.start()
    for copy in copies:
        copy.wait()


def per_device(diag_blocks, x_coupling, y_coupling, levels, listed):
    w = diag_blocks.shape[-1]
    sizes = (lax.axis_size("space"), lax.axis_size("grp"))
    nb = 4 if sizes[1] == 2 else 5
    n = nb * w
    half = w // 2 + 8
    block = jax.ShapeDtypeStruct((1, 1, w, w), F32)
    any_spec = pl.BlockSpec(memory_space=pl.ANY)
    vmem_spec = pl.BlockSpec(memory_space=pltpu.VMEM)
    results = pl.pallas_call(
        functools.partial(kernel, sizes),
        out_shape=pltpu.VMEM((3, w, w), F32),
        in_specs=[any_spec] * 5,
        out_specs=vmem_spec,
        scratch_shapes=[
            pltpu.VMEM((w, w), F32),
            pltpu.VMEM((w, w), F32),
            pltpu.VMEM((w, w), F32),
            pltpu.VMEM((1, w), F32),
            pltpu.SMEM((1, 2), jnp.int32),
            pltpu.SemaphoreType.DMA((5,)),
            pltpu.VMEM((2, w, w), F32),
            pltpu.VMEM((half, w), F32),
            pltpu.VMEM((half, w), F32),
            pltpu.VMEM((nb - 1, half, w), F32),
            pltpu.VMEM((2, w, w), F32),
            pltpu.VMEM((nb - 1, half, w), F32),
            pltpu.VMEM((nb - 1, w, w), F32),
            pltpu.VMEM((2, w, w), F32),
            pltpu.VMEM((n, n), BF16),
            pltpu.VMEM((n, w), F32),
            pltpu.VMEM((n, n), BF16),
            pltpu.VMEM((n, n), BF16),
            pltpu.VMEM((n, w), F32),
            pltpu.VMEM((n, w), F32),
            pltpu.VMEM((n, 2 * w), BF16),
            pltpu.VMEM((2, n, w), F32),
            pltpu.VMEM((nb - 1, w, w), F32),
            pltpu.SemaphoreType.DMA((16,)),
            pltpu.SemaphoreType.DMA((16,)),
        ],
        compiler_params=pltpu.CompilerParams(collective_id=0, has_side_effects=True),
    )(diag_blocks, x_coupling, y_coupling, levels, listed)
    return pl.pallas_call(
        write_out,
        out_shape=(block, block, block),
        in_specs=[vmem_spec],
        out_specs=(any_spec,) * 3,
        scratch_shapes=[pltpu.SemaphoreType.DMA((3,))],
    )(pltpu.with_memory_space_constraint(results, pltpu.VMEM))


def solution(mesh):
    blocks = P("space", "grp", None, None)
    rows = P("space", "grp", None)
    return jax.shard_map(
        per_device,
        mesh=mesh,
        in_specs=(blocks, blocks, blocks, rows, rows),
        out_specs=(blocks, blocks, blocks),
        check_vma=False,
    )
```

```python
import functools

import jax
import jax.numpy as jnp
from jax import lax
from jax.experimental import pallas as pl
from jax.experimental.pallas import tpu as pltpu
from jax.sharding import PartitionSpec as P

hubbard = 1.0
MESH = pl.DeviceIdType.MESH
F32 = jnp.float32
BF16 = jnp.bfloat16
K1, K3, K5, K7, K9 = -1.125, 1.21875, -0.84375, 0.28125, -0.03125


def mm(a, b):
    return jnp.dot(a, b, preferred_element_type=F32)


def iotas(shape):
    return lax.broadcasted_iota(jnp.int32, shape, 0), lax.broadcasted_iota(jnp.int32, shape, 1)


def eye(w):
    i, l = iotas((w, w))
    return i == l


def pack(m):
    w = m.shape[0]
    h = w // 2
    i, l = iotas((h, w))
    d = l - i
    top, low = m[:h], m[h:]
    rows = jnp.where((d >= 0) & (d < h), top, low)
    rows = jnp.where((d == 0) | (d == h), 0.5 * rows, rows)
    across = jnp.sum(jnp.where(d == h, top, 0.0), axis=0, keepdims=True)
    return rows, jnp.broadcast_to(across, (8, w))


def unpack(p):
    w = p.shape[1]
    h = w // 2
    i, l = iotas((h, w))
    d = l - i
    inside = (d >= 0) & (d < h)
    rows = p[:h]
    across = jnp.broadcast_to(p[h : h + 1], (h, w))
    top = jnp.where(inside, rows, jnp.where(d == h, across, 0.0))
    low = jnp.where(inside, 0.0, rows)
    half = jnp.concatenate([top, low], axis=0)
    return half + half.T


def square(nb, w, am, sx):
    for i in range(0, nb, 2):
        tile = slice(i * w, min(i + 2, nb) * w)
        sx[:, tile] = mm(am[...], am[:, tile]).astype(BF16)


def square_early(w, am, sx, s00):
    e = slice(0, 3 * w)
    part = mm(am[e, e], am[e, e])
    sx[e, e] = part.astype(BF16)
    s00[...] = part[:w, :w]


def square_couplings(nb, w, am, sx, s00, rows, tops):
    def bl(i):
        return slice(i * w, (i + 1) * w)

    total = s00[...]
    for s in range(3, nb):
        total = total + mm(am[bl(0), bl(s)], am[bl(s), bl(0)])
        row = mm(am[bl(s), bl(0)], am[bl(0), :])
        rows[s - 3, :, :w] = row[:, bl(0)]
        rows[s - 3, :, w:] = row[:, bl(s)]
        col = mm(am[: 3 * w, bl(0)], am[bl(0), bl(s)])
        tops[s - 3] = col[bl(0), :]
        for r in range(1, nb):
            if r != s:
                sx[bl(s), bl(r)] = row[:, bl(r)].astype(BF16)
        sx[w : 3 * w, bl(s)] = col[w:, :].astype(BF16)
    sx[bl(0), bl(0)] = total.astype(BF16)


def square_diagonals(nb, w, am, sx, rows, tops):
    def bl(i):
        return slice(i * w, (i + 1) * w)

    for s in range(3, nb):
        diag = am[bl(s), bl(s)]
        row = rows[s - 3] + mm(diag, jnp.concatenate([am[bl(s), bl(0)], diag], axis=1))
        sx[bl(s), bl(0)] = row[:, :w].astype(BF16)
        sx[bl(s), bl(s)] = row[:, w:].astype(BF16)
        sx[bl(0), bl(s)] = (tops[s - 3] + mm(am[bl(0), bl(s)], diag)).astype(BF16)


def powers(nb, w, am, sx, fb, v3f, v5f, vb):
    n = nb * w
    at = nb // 2 * w
    halves = (slice(0, at), slice(at, n))

    def bl(i):
        return slice(i * w, (i + 1) * w)

    squares = [jnp.zeros((8, w), F32)]

    def keep_fourth(rows, j, f):
        fb[rows, bl(j)] = f.astype(BF16)
        squares[0] = squares[0] + jnp.sum((f * f).reshape(-1, 8, w), axis=0)

    right = jnp.concatenate([sx[:, bl(0)], am[:, bl(0)]], axis=1)
    for rows in halves:
        r = mm(sx[rows, :], right)
        keep_fourth(rows, 0, r[:, :w])
        v3f[rows, :] = r[:, w:]
        vb[rows, :w] = r[:, w:].astype(BF16)
    last = nb - 1
    for i in range(1, last, 2):
        pair = [i] if i == last else [i, i + 1]
        right = sx[:, i * w : (i + len(pair)) * w]
        for rows in halves:
            r = mm(sx[rows, :], right)
            for at, j in enumerate(pair):
                keep_fourth(rows, j, r[:, bl(at)])
    right = vb[:, :w]
    if nb % 2 == 0:
        right = jnp.concatenate([sx[:, bl(last)], right], axis=1)
    for rows in halves:
        r = mm(sx[rows, :], right)
        if nb % 2 == 0:
            keep_fourth(rows, last, r[:, :w])
        v5 = r[:, -w:]
        v5f[rows, :] = v5
        vb[rows, w:] = v5.astype(BF16)
    return jnp.sum(jnp.sum(squares[0], axis=1, keepdims=True), axis=0, keepdims=True)


def coefficients(total):
    r = lax.rsqrt(lax.rsqrt(lax.rsqrt(total + 1e-06)))
    r2 = r * r
    r3 = r2 * r
    r4 = r2 * r2
    return K1 * r, K3 * r3, K5 * (r4 * r), K7 * (r4 * r3), K9 * (r4 * r4 * r)


def kernel(
    sizes, diag_hbm, x_hbm, y_hbm, lev_hbm, list_hbm, out_ref,
    din, xin, yin, lin, fin, in_sems,
    coup_out, diag_out, diag_out2, rd1, rb1, rd2, rc2, rf3,
    am, v1f, sx, s00, rows, tops, fb, v3f, v5f, vb, cols, rowf,
    send_sems, recv_sems,
):
    nx, ny = sizes
    w = din.shape[0]
    h = w // 2
    merged = ny == 2
    nb = 4 if merged else 5
    ix = lax.axis_index("space")
    iy = lax.axis_index("grp")
    even = lax.rem(ix, 2) == 0
    odd = jnp.logical_not(even)

    def bl(i):
        return slice(i * w, (i + 1) * w)

    def pick(a, b):
        return jnp.where(even, a, b)

    last_x, last_y = ix == nx - 1, iy == ny - 1
    here = [
        jnp.logical_or(odd, jnp.logical_not(last_x)),
        jnp.where(even, ix > 0, jnp.logical_not(last_x)),
    ]
    where_x = [jnp.where(even, ix + 1, ix - 1), jnp.where(even, ix - 1, ix + 1)]
    device = [(jnp.clip(at, 0, nx - 1), iy) for at in where_x]
    upper = [even, odd]
    if merged:
        here.append(jnp.logical_or(iy > 0, jnp.logical_not(last_y)))
        device.append((ix, jnp.where(last_y, iy - 1, iy + 1)))
        upper.append(jnp.logical_not(last_y))
    else:
        here += [iy > 0, jnp.logical_not(last_y)]
        device += [(ix, jnp.maximum(iy - 1, 0)), (ix, jnp.minimum(iy + 1, ny - 1))]
        upper += [iy < 0, iy >= 0]
    peer_role = (0, 1, 2) if merged else (0, 1, 3, 2)
    axis_of = (0, 0, 1) if merged else (0, 0, 1, 1)
    grp_last = jnp.logical_or(even, last_y)
    if merged:
        both = lambda vs: [None, vs[0], jnp.where(grp_last, vs[1], vs[2]), jnp.where(grp_last, vs[2], vs[1])]
    else:
        both = lambda vs: [None, *vs]
    role, peer, axis = both((0, 1, 2, 3)[: nb - 1]), both(peer_role), both(axis_of)
    has, up = both(here), both(upper)
    dev_x, dev_y = both([d[0] for d in device]), both([d[1] for d in device])
    slot_x = pick(1, jnp.where(grp_last, 2, 3) if merged else 2)
    slot_y = jnp.where(grp_last, 3, 2) if merged else 4
    slots = range(1, nb)

    barrier = pltpu.get_barrier_semaphore()
    for s in slots:
        @pl.when(has[s])
        def _():
            pl.semaphore_signal(barrier, inc=1, device_id=(dev_x[s], dev_y[s]), device_id_type=MESH)

    loads = [
        pltpu.make_async_copy(diag_hbm.at[0, 0], din, in_sems.at[0]),
        pltpu.make_async_copy(lev_hbm.at[0], lin, in_sems.at[3]),
        pltpu.make_async_copy(list_hbm.at[0], fin, in_sems.at[4]),
        pltpu.make_async_copy(y_hbm.at[0, 0], yin, in_sems.at[2]),
        pltpu.make_async_copy(x_hbm.at[0, 0], xin, in_sems.at[1]),
    ]
    for load in loads:
        load.start()
    for s in slots:
        @pl.when(jnp.logical_not(has[s]))
        def _():
            rd1[role[s]] = jnp.zeros((h + 8, w), F32)
            rb1[role[s]] = jnp.zeros((w, w), F32)
            rd2[role[s]] = jnp.zeros((h + 8, w), F32)
            rc2[role[s]] = jnp.zeros((w, w), F32)
    for a, last in enumerate((last_x, last_y)):
        @pl.when(last)
        def _():
            rf3[a] = jnp.zeros((w, w), F32)
    for i in slots:
        for j in slots:
            if i != j:
                am[bl(i), bl(j)] = jnp.zeros((w, w), BF16)
    for load in loads:
        load.wait()
    one_eye = eye(w)
    flag_x = fin[0, 0].astype(F32) * (ix < nx - 1).astype(F32)
    flag_y = fin[0, 1].astype(F32) * (iy < ny - 1).astype(F32)
    raw = din[...]
    onsite = 0.5 * (raw + raw.T) + jnp.where(one_eye, jnp.broadcast_to(lin[...], (w, w)), 0.0)
    diag_out[:h], diag_out[h:] = pack(onsite)
    coup_out[0] = xin[...] * flag_x
    coup_out[1] = yin[...] * flag_y

    count = sum(has[s].astype(jnp.int32) for s in slots)
    pl.semaphore_wait(barrier, count)

    def transfer(src, dst, s, index_send, index_recv):
        return pltpu.make_async_remote_copy(
            src_ref=src, dst_ref=dst, send_sem=send_sems.at[index_send],
            recv_sem=recv_sems.at[index_recv], device_id=(dev_x[s], dev_y[s]), device_id_type=MESH,
        )

    def diag1(s, at):
        return transfer(diag_out, rd1.at[at[s]], s, role[s], at[s])

    def coup1(s, at):
        return transfer(coup_out.at[axis[s]], rb1.at[at[s]], s, 4 + axis[s], 4 + axis[s])

    def diag2(s, at):
        return transfer(diag_out2, rd2.at[at[s]], s, 6 + role[s], 6 + at[s])

    def coup2(s, at):
        return transfer(cols.at[0, s], rc2.at[at[s]], s, 10 + role[s], 10 + at[s])

    def coup3(s, at):
        return transfer(cols.at[1, s], rf3.at[axis[s]], s, 14 + axis[s], 14 + axis[s])

    def sends(make, s):
        if make is coup1:
            return jnp.logical_and(has[s], up[s])
        if make is coup3:
            return jnp.logical_and(has[s], jnp.logical_not(up[s]))
        return has[s]

    def hears(make, s):
        if make is coup1:
            return jnp.logical_and(has[s], jnp.logical_not(up[s]))
        if make is coup3:
            return jnp.logical_and(has[s], up[s])
        return has[s]

    def start(*copies, only=None):
        for make, s in copies:
            there = sends(make, s) if only is None else jnp.logical_and(sends(make, s), only)

            @pl.when(there)
            def _():
                make(s, peer).start()

    def wait_recv(*copies):
        for make, s in copies:
            @pl.when(hears(make, s))
            def _():
                make(s, role).wait_recv()

    late_first = tuple(range(nb - 1, 0, -1))
    for s in late_first:
        start((coup1, s), (diag1, s))

    am[bl(0), bl(0)] = onsite.astype(BF16)
    v1f[bl(0), :] = onsite
    for a, (last, s) in enumerate(((last_x, slot_x), (last_y, slot_y))):
        @pl.when(jnp.logical_not(last))
        def _():
            rb1[pick(0, 1) if a == 0 else nb - 2] = coup_out[a].T

    def hear1(s):
        wait_recv((coup1, s), (diag1, s))
        col = rb1[role[s]]
        am[bl(0), bl(s)] = col.T.astype(BF16)
        am[bl(s), bl(0)] = col.astype(BF16)
        v1f[bl(s), :] = col
        am[bl(s), bl(s)] = unpack(rd1[role[s]]).astype(BF16)

    for s in slots:
        hear1(s)
    square(nb, w, am, sx)
    total = powers(nb, w, am, sx, fb, v3f, v5f, vb)
    c1, c3, c5, c7, c9 = coefficients(total)

    def finish(step, *blocks):
        for s in blocks:
            for at in ((0, h), (h, w)) if len(blocks) == 1 else ((0, w),):
                r = slice(s * w + at[0], s * w + at[1])
                v79 = mm(fb[r, :], vb[...])
                low = c1 * v1f[r, :] + c3 * v3f[r, :] + c5 * v5f[r, :]
                cols[step, s, at[0] : at[1], :] = low + c7 * v79[:, :w] + c9 * v79[:, w:]

    tail = tuple(range(nb - 1, 1, -1))
    finish(0, *tail)
    start(*((coup2, s) for s in tail))
    finish(0, 0, 1)
    start((coup2, 1))
    c0 = cols[0, 0]
    two = v1f[bl(0), :] + (0.5 * hubbard) * (c0 + c0.T)
    diag_out2[:h], diag_out2[h:] = pack(two)
    start(*((diag2, s) for s in late_first))

    am[bl(0), bl(0)] = two.astype(BF16)
    v1f[bl(0), :] = two
    for s in slots:
        rowf[s - 1] = (v1f[bl(s), :] + (0.5 * hubbard) * cols[0, s]).T

    def coupling2(s):
        row = rowf[s - 1] + (0.5 * hubbard) * rc2[role[s]]
        col = row.T
        am[bl(0), bl(s)] = row.astype(BF16)
        am[bl(s), bl(0)] = col.astype(BF16)
        v1f[bl(s), :] = col

    for s in (1, 2):
        wait_recv((coup2, s), (diag2, s))
        coupling2(s)
        am[bl(s), bl(s)] = unpack(rd2[role[s]]).astype(BF16)
    square_early(w, am, sx, s00)
    wait_recv(*((coup2, s) for s in range(3, nb)))
    for s in range(3, nb):
        coupling2(s)
    square_couplings(nb, w, am, sx, s00, rows, tops)
    wait_recv(*((diag2, s) for s in range(3, nb)))
    for s in range(3, nb):
        am[bl(s), bl(s)] = unpack(rd2[role[s]]).astype(BF16)
    square_diagonals(nb, w, am, sx, rows, tops)

    total = powers(nb, w, am, sx, fb, v3f, v5f, vb)
    c1, c3, c5, c7, c9 = coefficients(total)
    finish(1, *tail)
    start((coup3, 2), (coup3, 3))
    finish(1, 0, 1)
    start((coup3, 1))
    c0 = cols[1, 0]
    out_ref[0] = 0.5 * (c0 + c0.T) + jnp.where(one_eye, 0.5, 0.0)
    half_x = 0.5 * cols[1, slot_x].T
    half_y = jnp.where(last_y, 0.0, 0.5 * cols[1, slot_y].T)
    wait_recv(*((coup3, s) for s in slots))
    out_ref[1] = half_x + 0.5 * rf3[0]
    out_ref[2] = half_y + 0.5 * rf3[1]
    for make in (diag1, coup1, coup2, diag2, coup3):
        for s in slots:
            @pl.when(sends(make, s))
            def _():
                make(s, peer).wait_send()


def write_out(in_ref, od_ref, ox_ref, oy_ref, sems):
    copies = [
        pltpu.make_async_copy(in_ref.at[i], ref.at[0, 0], sems.at[i])
        for i, ref in enumerate((od_ref, ox_ref, oy_ref))
    ]
    for copy in copies:
        copy.start()
    for copy in copies:
        copy.wait()


def per_device(diag_blocks, x_coupling, y_coupling, levels, listed):
    w = diag_blocks.shape[-1]
    sizes = (lax.axis_size("space"), lax.axis_size("grp"))
    nb = 4 if sizes[1] == 2 else 5
    n = nb * w
    half = w // 2 + 8
    block = jax.ShapeDtypeStruct((1, 1, w, w), F32)
    any_spec = pl.BlockSpec(memory_space=pl.ANY)
    vmem_spec = pl.BlockSpec(memory_space=pltpu.VMEM)
    results = pl.pallas_call(
        functools.partial(kernel, sizes),
        out_shape=pltpu.VMEM((3, w, w), F32),
        in_specs=[any_spec] * 5,
        out_specs=vmem_spec,
        scratch_shapes=[
            pltpu.VMEM((w, w), F32),
            pltpu.VMEM((w, w), F32),
            pltpu.VMEM((w, w), F32),
            pltpu.VMEM((1, w), F32),
            pltpu.SMEM((1, 2), jnp.int32),
            pltpu.SemaphoreType.DMA((5,)),
            pltpu.VMEM((2, w, w), F32),
            pltpu.VMEM((half, w), F32),
            pltpu.VMEM((half, w), F32),
            pltpu.VMEM((nb - 1, half, w), F32),
            pltpu.VMEM((nb - 1, w, w), F32),
            pltpu.VMEM((nb - 1, half, w), F32),
            pltpu.VMEM((nb - 1, w, w), F32),
            pltpu.VMEM((2, w, w), F32),
            pltpu.VMEM((n, n), BF16),
            pltpu.VMEM((n, w), F32),
            pltpu.VMEM((n, n), BF16),
            pltpu.VMEM((w, w), F32),
            pltpu.VMEM((nb - 3, w, 2 * w), F32),
            pltpu.VMEM((nb - 3, w, w), F32),
            pltpu.VMEM((n, n), BF16),
            pltpu.VMEM((n, w), F32),
            pltpu.VMEM((n, w), F32),
            pltpu.VMEM((n, 2 * w), BF16),
            pltpu.VMEM((2, nb, w, w), F32),
            pltpu.VMEM((nb - 1, w, w), F32),
            pltpu.SemaphoreType.DMA((16,)),
            pltpu.SemaphoreType.DMA((16,)),
        ],
        compiler_params=pltpu.CompilerParams(collective_id=0, has_side_effects=True),
    )(diag_blocks, x_coupling, y_coupling, levels, listed)
    return pl.pallas_call(
        write_out,
        out_shape=(block, block, block),
        in_specs=[vmem_spec],
        out_specs=(any_spec,) * 3,
        scratch_shapes=[pltpu.SemaphoreType.DMA((3,))],
    )(pltpu.with_memory_space_constraint(results, pltpu.VMEM))


def solution(mesh):
    blocks = P("space", "grp", None, None)
    rows = P("space", "grp", None)
    return jax.shard_map(
        per_device,
        mesh=mesh,
        in_specs=(blocks, blocks, blocks, rows, rows),
        out_specs=(blocks, blocks, blocks),
        check_vma=False,
    )
```

```python
import functools

import jax
import jax.numpy as jnp
from jax import lax
from jax.experimental import pallas as pl
from jax.experimental.pallas import tpu as pltpu
from jax.sharding import PartitionSpec as P

hubbard = 1.0
MESH = pl.DeviceIdType.MESH
F32 = jnp.float32
BF16 = jnp.bfloat16
K1, K3, K5, K7, K9 = -1.125, 1.21875, -0.84375, 0.28125, -0.03125


def mm(a, b):
    return jnp.dot(a, b, preferred_element_type=F32)


def iotas(shape):
    return lax.broadcasted_iota(jnp.int32, shape, 0), lax.broadcasted_iota(jnp.int32, shape, 1)


def eye(w):
    i, l = iotas((w, w))
    return i == l


def pack(m):
    w = m.shape[0]
    h = w // 2
    i, l = iotas((h, w))
    d = l - i
    top, low = m[:h], m[h:]
    rows = jnp.where((d >= 0) & (d < h), top, low)
    rows = jnp.where((d == 0) | (d == h), 0.5 * rows, rows)
    across = jnp.sum(jnp.where(d == h, top, 0.0), axis=0, keepdims=True)
    return rows, jnp.broadcast_to(across, (8, w))


def unpack(p):
    w = p.shape[1]
    h = w // 2
    i, l = iotas((h, w))
    d = l - i
    inside = (d >= 0) & (d < h)
    rows = p[:h]
    across = jnp.broadcast_to(p[h : h + 1], (h, w))
    top = jnp.where(inside, rows, jnp.where(d == h, across, 0.0))
    low = jnp.where(inside, 0.0, rows)
    half = jnp.concatenate([top, low], axis=0).astype(BF16)
    return half + half.T


def side(ref, which, rows=slice(None)):
    return jnp.concatenate([ref[j, rows, :] for j in which], axis=1)


def depth_order(nb):
    return (1, 2, 0, *range(3, nb))


def right_side(nb, w, columns):
    parts = [[ref[j, k * w : (k + 1) * w, :] for ref, j in columns] for k in depth_order(nb)]
    return jnp.concatenate([jnp.concatenate(part, axis=1) for part in parts], axis=0)


def square(nb, w, am, sx):
    for i in range(0, nb, 2):
        pair = range(i, min(i + 2, nb))
        part = mm(side(am, depth_order(nb)), right_side(nb, w, [(am, j) for j in pair]))
        for at, j in enumerate(pair):
            sx[j] = part[:, at * w : (at + 1) * w].astype(BF16)


def square_early(w, am, sx, s00):
    e = slice(0, 3 * w)
    own = side(am, range(3), e)
    part = mm(own, own)
    for j in range(3):
        sx[j, e, :] = part[:, j * w : (j + 1) * w].astype(BF16)
    s00[...] = part[:w, :w]


def square_couplings(nb, w, am, sx, s00, rows, tops):
    def bl(i):
        return slice(i * w, (i + 1) * w)

    total = s00[...]
    for s in range(3, nb):
        total = total + mm(am[s, bl(0), :], am[0, bl(s), :])
        row = mm(am[0, bl(s), :], side(am, range(nb), bl(0)))
        rows[s - 3, :, :w] = row[:, bl(0)]
        rows[s - 3, :, w:] = row[:, bl(s)]
        col = mm(am[0, : 3 * w, :], am[s, bl(0), :])
        tops[s - 3] = col[bl(0), :]
        for r in range(1, nb):
            if r != s:
                sx[r, bl(s), :] = row[:, bl(r)].astype(BF16)
        sx[s, w : 3 * w, :] = col[w:, :].astype(BF16)
    sx[0, bl(0), :] = total.astype(BF16)


def square_diagonals(nb, w, am, sx, rows, tops):
    def bl(i):
        return slice(i * w, (i + 1) * w)

    for s in range(3, nb):
        diag = am[s, bl(s), :]
        row = rows[s - 3] + mm(diag, jnp.concatenate([am[0, bl(s), :], diag], axis=1))
        sx[0, bl(s), :] = row[:, :w].astype(BF16)
        sx[s, bl(s), :] = row[:, w:].astype(BF16)
        sx[s, bl(0), :] = (tops[s - 3] + mm(am[s, bl(0), :], diag)).astype(BF16)


def powers(nb, w, am, sx, fb, v3f, v5f, vb):
    n = nb * w
    at = nb // 2 * w
    halves = (slice(0, at), slice(at, n))

    def bl(i):
        return slice(i * w, (i + 1) * w)

    squares = [jnp.zeros((8, w), F32)]

    def keep_fourth(rows, j, f):
        fb[j, rows, :] = f.astype(BF16)
        squares[0] = squares[0] + jnp.sum((f * f).reshape(-1, 8, w), axis=0)

    right = right_side(nb, w, [(sx, 0), (am, 0)])
    for rows in halves:
        r = mm(side(sx, depth_order(nb), rows), right)
        keep_fourth(rows, 0, r[:, :w])
        v3f[rows, :] = r[:, w:]
        vb[0, rows, :] = r[:, w:].astype(BF16)
    last = nb - 1
    for i in range(1, last, 2):
        pair = [i] if i == last else [i, i + 1]
        right = right_side(nb, w, [(sx, j) for j in pair])
        for rows in halves:
            r = mm(side(sx, depth_order(nb), rows), right)
            for at, j in enumerate(pair):
                keep_fourth(rows, j, r[:, bl(at)])
    right = right_side(nb, w, [(sx, last), (vb, 0)] if nb % 2 == 0 else [(vb, 0)])
    for rows in halves:
        r = mm(side(sx, depth_order(nb), rows), right)
        if nb % 2 == 0:
            keep_fourth(rows, last, r[:, :w])
        v5 = r[:, -w:]
        v5f[rows, :] = v5
        vb[1, rows, :] = v5.astype(BF16)
    return jnp.sum(jnp.sum(squares[0], axis=1, keepdims=True), axis=0, keepdims=True)


def coefficients(total):
    r = lax.rsqrt(lax.rsqrt(lax.rsqrt(total + 1e-06)))
    r2 = r * r
    r3 = r2 * r
    r4 = r2 * r2
    return K1 * r, K3 * r3, K5 * (r4 * r), K7 * (r4 * r3), K9 * (r4 * r4 * r)


def kernel(
    sizes, diag_hbm, x_hbm, y_hbm, lev_hbm, list_hbm, out_ref,
    din, xin, yin, lin, fin, in_sems,
    coup_out, diag_out, diag_out2, rd1, rb1, rd2, rc2, rf3,
    am, v1f, sx, s00, rows, tops, fb, v3f, v5f, vb, cols, rowf,
    send_sems, recv_sems,
):
    nx, ny = sizes
    w = din.shape[0]
    h = w // 2
    merged = ny == 2
    nb = 4 if merged else 5
    ix = lax.axis_index("space")
    iy = lax.axis_index("grp")
    even = lax.rem(ix, 2) == 0
    odd = jnp.logical_not(even)

    def bl(i):
        return slice(i * w, (i + 1) * w)

    def pick(a, b):
        return jnp.where(even, a, b)

    last_x, last_y = ix == nx - 1, iy == ny - 1
    here = [
        jnp.logical_or(odd, jnp.logical_not(last_x)),
        jnp.where(even, ix > 0, jnp.logical_not(last_x)),
    ]
    where_x = [jnp.where(even, ix + 1, ix - 1), jnp.where(even, ix - 1, ix + 1)]
    device = [(jnp.clip(at, 0, nx - 1), iy) for at in where_x]
    upper = [even, odd]
    if merged:
        here.append(jnp.logical_or(iy > 0, jnp.logical_not(last_y)))
        device.append((ix, jnp.where(last_y, iy - 1, iy + 1)))
        upper.append(jnp.logical_not(last_y))
    else:
        here += [iy > 0, jnp.logical_not(last_y)]
        device += [(ix, jnp.maximum(iy - 1, 0)), (ix, jnp.minimum(iy + 1, ny - 1))]
        upper += [iy < 0, iy >= 0]
    peer_role = (0, 1, 2) if merged else (0, 1, 3, 2)
    axis_of = (0, 0, 1) if merged else (0, 0, 1, 1)
    grp_last = jnp.logical_or(even, last_y)
    if merged:
        both = lambda vs: [None, vs[0], jnp.where(grp_last, vs[1], vs[2]), jnp.where(grp_last, vs[2], vs[1])]
    else:
        both = lambda vs: [None, *vs]
    role, peer, axis = both((0, 1, 2, 3)[: nb - 1]), both(peer_role), both(axis_of)
    has, up = both(here), both(upper)
    dev_x, dev_y = both([d[0] for d in device]), both([d[1] for d in device])
    slot_x = pick(1, jnp.where(grp_last, 2, 3) if merged else 2)
    slot_y = jnp.where(grp_last, 3, 2) if merged else 4
    slots = range(1, nb)

    barrier = pltpu.get_barrier_semaphore()
    loads = [
        pltpu.make_async_copy(diag_hbm.at[0, 0], din, in_sems.at[0]),
        pltpu.make_async_copy(lev_hbm.at[0], lin, in_sems.at[3]),
        pltpu.make_async_copy(list_hbm.at[0], fin, in_sems.at[4]),
        pltpu.make_async_copy(y_hbm.at[0, 0], yin, in_sems.at[2]),
        pltpu.make_async_copy(x_hbm.at[0, 0], xin, in_sems.at[1]),
    ]
    for load in loads:
        load.start()
    for s in slots:
        @pl.when(has[s])
        def _():
            pl.semaphore_signal(barrier, inc=1, device_id=(dev_x[s], dev_y[s]), device_id_type=MESH)

    for s in slots:
        @pl.when(jnp.logical_not(has[s]))
        def _():
            rd1[role[s]] = jnp.zeros((h + 8, w), F32)
            rb1[role[s]] = jnp.zeros((w, w), F32)
            rd2[role[s]] = jnp.zeros((h + 8, w), F32)
            rc2[role[s]] = jnp.zeros((w, w), F32)
    for a, last in enumerate((last_x, last_y)):
        @pl.when(last)
        def _():
            rf3[a] = jnp.zeros((w, w), F32)
    for i in slots:
        for j in slots:
            if i != j:
                am[j, bl(i), :] = jnp.zeros((w, w), BF16)
    for load in loads:
        load.wait()
    one_eye = eye(w)
    flag_x = fin[0, 0].astype(F32) * (ix < nx - 1).astype(F32)
    flag_y = fin[0, 1].astype(F32) * (iy < ny - 1).astype(F32)
    raw = din[...]
    onsite = 0.5 * (raw + raw.T) + jnp.where(one_eye, jnp.broadcast_to(lin[...], (w, w)), 0.0)
    diag_out[:h], diag_out[h:] = pack(onsite)
    coup_out[0] = xin[...] * flag_x
    coup_out[1] = yin[...] * flag_y

    count = sum(has[s].astype(jnp.int32) for s in slots)
    pl.semaphore_wait(barrier, count)

    def transfer(src, dst, s, index_send, index_recv):
        return pltpu.make_async_remote_copy(
            src_ref=src, dst_ref=dst, send_sem=send_sems.at[index_send],
            recv_sem=recv_sems.at[index_recv], device_id=(dev_x[s], dev_y[s]), device_id_type=MESH,
        )

    def diag1(s, at):
        return transfer(diag_out, rd1.at[at[s]], s, role[s], at[s])

    def coup1(s, at):
        return transfer(coup_out.at[axis[s]], rb1.at[at[s]], s, 4 + axis[s], 4 + axis[s])

    def diag2(s, at):
        return transfer(diag_out2, rd2.at[at[s]], s, 6 + role[s], 6 + at[s])

    def coup2(s, at):
        return transfer(cols.at[0, s], rc2.at[at[s]], s, 10 + role[s], 10 + at[s])

    def coup3(s, at):
        return transfer(cols.at[1, s], rf3.at[axis[s]], s, 14 + axis[s], 14 + axis[s])

    def sends(make, s):
        if make is coup1:
            return jnp.logical_and(has[s], up[s])
        if make is coup3:
            return jnp.logical_and(has[s], jnp.logical_not(up[s]))
        return has[s]

    def hears(make, s):
        if make is coup1:
            return jnp.logical_and(has[s], jnp.logical_not(up[s]))
        if make is coup3:
            return jnp.logical_and(has[s], up[s])
        return has[s]

    def start(*copies, only=None):
        for make, s in copies:
            there = sends(make, s) if only is None else jnp.logical_and(sends(make, s), only)

            @pl.when(there)
            def _():
                make(s, peer).start()

    def wait_recv(*copies):
        for make, s in copies:
            @pl.when(hears(make, s))
            def _():
                make(s, role).wait_recv()

    late_first = tuple(range(nb - 1, 0, -1))
    for s in late_first:
        start((coup1, s), (diag1, s))

    am[0, bl(0), :] = onsite.astype(BF16)
    v1f[bl(0), :] = onsite
    for a, (last, s) in enumerate(((last_x, slot_x), (last_y, slot_y))):
        @pl.when(jnp.logical_not(last))
        def _():
            rb1[pick(0, 1) if a == 0 else nb - 2] = coup_out[a].T

    def hear1(s):
        wait_recv((coup1, s), (diag1, s))
        col = rb1[role[s]]
        half = col.astype(BF16)
        am[s, bl(0), :] = half.T
        am[0, bl(s), :] = half
        v1f[bl(s), :] = col
        am[s, bl(s), :] = unpack(rd1[role[s]])

    for s in slots:
        hear1(s)
    square(nb, w, am, sx)
    total = powers(nb, w, am, sx, fb, v3f, v5f, vb)
    c1, c3, c5, c7, c9 = coefficients(total)

    def finish(step, *blocks):
        for s in blocks:
            for at in ((0, h), (h, w)) if len(blocks) == 1 else ((0, w),):
                r = slice(s * w + at[0], s * w + at[1])
                v79 = mm(side(fb, range(nb), r), side(vb, range(2)))
                low = c1 * v1f[r, :] + c3 * v3f[r, :] + c5 * v5f[r, :]
                cols[step, s, at[0] : at[1], :] = low + c7 * v79[:, :w] + c9 * v79[:, w:]

    tail = tuple(range(nb - 1, 1, -1))
    finish(0, *tail)
    start(*((coup2, s) for s in tail))
    finish(0, 0, 1)
    start((coup2, 1))
    c0 = cols[0, 0]
    two = v1f[bl(0), :] + (0.5 * hubbard) * (c0 + c0.T)
    diag_out2[:h], diag_out2[h:] = pack(two)
    start(*((diag2, s) for s in late_first))

    am[0, bl(0), :] = two.astype(BF16)
    v1f[bl(0), :] = two
    for s in slots:
        rowf[s - 1] = (v1f[bl(s), :] + (0.5 * hubbard) * cols[0, s]).T

    def coupling2(s):
        row = rowf[s - 1] + (0.5 * hubbard) * rc2[role[s]]
        half = row.astype(BF16)
        am[s, bl(0), :] = half
        am[0, bl(s), :] = half.T
        v1f[bl(s), :] = row.T

    for s in (1, 2):
        wait_recv((coup2, s), (diag2, s))
        coupling2(s)
        am[s, bl(s), :] = unpack(rd2[role[s]])
    square_early(w, am, sx, s00)
    wait_recv(*((coup2, s) for s in range(3, nb)))
    for s in range(3, nb):
        coupling2(s)
    square_couplings(nb, w, am, sx, s00, rows, tops)
    wait_recv(*((diag2, s) for s in range(3, nb)))
    for s in range(3, nb):
        am[s, bl(s), :] = unpack(rd2[role[s]])
    square_diagonals(nb, w, am, sx, rows, tops)

    total = powers(nb, w, am, sx, fb, v3f, v5f, vb)
    c1, c3, c5, c7, c9 = coefficients(total)
    finish(1, *tail)
    start((coup3, 2), (coup3, 3))
    finish(1, 0, 1)
    start((coup3, 1))
    c0 = cols[1, 0]
    out_ref[0] = 0.5 * (c0 + c0.T) + jnp.where(one_eye, 0.5, 0.0)
    half_x = 0.5 * cols[1, slot_x].T
    half_y = jnp.where(last_y, 0.0, 0.5 * cols[1, slot_y].T)
    wait_recv(*((coup3, s) for s in slots))
    out_ref[1] = half_x + 0.5 * rf3[0]
    out_ref[2] = half_y + 0.5 * rf3[1]
    for make in (diag1, coup1, coup2, diag2, coup3):
        for s in slots:
            @pl.when(sends(make, s))
            def _():
                make(s, peer).wait_send()


def write_out(in_ref, od_ref, ox_ref, oy_ref, sems):
    copies = [
        pltpu.make_async_copy(in_ref.at[i], ref.at[0, 0], sems.at[i])
        for i, ref in enumerate((od_ref, ox_ref, oy_ref))
    ]
    for copy in copies:
        copy.start()
    for copy in copies:
        copy.wait()


def per_device(diag_blocks, x_coupling, y_coupling, levels, listed):
    w = diag_blocks.shape[-1]
    sizes = (lax.axis_size("space"), lax.axis_size("grp"))
    nb = 4 if sizes[1] == 2 else 5
    n = nb * w
    half = w // 2 + 8
    block = jax.ShapeDtypeStruct((1, 1, w, w), F32)
    any_spec = pl.BlockSpec(memory_space=pl.ANY)
    vmem_spec = pl.BlockSpec(memory_space=pltpu.VMEM)
    results = pl.pallas_call(
        functools.partial(kernel, sizes),
        out_shape=pltpu.VMEM((3, w, w), F32),
        in_specs=[any_spec] * 5,
        out_specs=vmem_spec,
        scratch_shapes=[
            pltpu.VMEM((w, w), F32),
            pltpu.VMEM((w, w), F32),
            pltpu.VMEM((w, w), F32),
            pltpu.VMEM((1, w), F32),
            pltpu.SMEM((1, 2), jnp.int32),
            pltpu.SemaphoreType.DMA((5,)),
            pltpu.VMEM((2, w, w), F32),
            pltpu.VMEM((half, w), F32),
            pltpu.VMEM((half, w), F32),
            pltpu.VMEM((nb - 1, half, w), F32),
            pltpu.VMEM((nb - 1, w, w), F32),
            pltpu.VMEM((nb - 1, half, w), F32),
            pltpu.VMEM((nb - 1, w, w), F32),
            pltpu.VMEM((2, w, w), F32),
            pltpu.VMEM((nb, n, w), BF16),
            pltpu.VMEM((n, w), F32),
            pltpu.VMEM((nb, n, w), BF16),
            pltpu.VMEM((w, w), F32),
            pltpu.VMEM((nb - 3, w, 2 * w), F32),
            pltpu.VMEM((nb - 3, w, w), F32),
            pltpu.VMEM((nb, n, w), BF16),
            pltpu.VMEM((n, w), F32),
            pltpu.VMEM((n, w), F32),
            pltpu.VMEM((2, n, w), BF16),
            pltpu.VMEM((2, nb, w, w), F32),
            pltpu.VMEM((nb - 1, w, w), F32),
            pltpu.SemaphoreType.DMA((16,)),
            pltpu.SemaphoreType.DMA((16,)),
        ],
        compiler_params=pltpu.CompilerParams(collective_id=0, has_side_effects=True),
    )(diag_blocks, x_coupling, y_coupling, levels, listed)
    return pl.pallas_call(
        write_out,
        out_shape=(block, block, block),
        in_specs=[vmem_spec],
        out_specs=(any_spec,) * 3,
        scratch_shapes=[pltpu.SemaphoreType.DMA((3,))],
    )(pltpu.with_memory_space_constraint(results, pltpu.VMEM))


def solution(mesh):
    blocks = P("space", "grp", None, None)
    rows = P("space", "grp", None)
    return jax.shard_map(
        per_device,
        mesh=mesh,
        in_specs=(blocks, blocks, blocks, rows, rows),
        out_specs=(blocks, blocks, blocks),
        check_vma=False,
    )
```

```python
import functools

import jax
import jax.numpy as jnp
from jax import lax
from jax.experimental import pallas as pl
from jax.experimental.pallas import tpu as pltpu
from jax.sharding import PartitionSpec as P

hubbard = 1.0
MESH = pl.DeviceIdType.MESH
F32 = jnp.float32
BF16 = jnp.bfloat16
K1, K3, K5, K7, K9 = -1.125, 1.21875, -0.84375, 0.28125, -0.03125


def mm(a, b):
    return jnp.dot(a, b, preferred_element_type=F32)


def iotas(shape):
    return lax.broadcasted_iota(jnp.int32, shape, 0), lax.broadcasted_iota(jnp.int32, shape, 1)


def eye(w):
    i, l = iotas((w, w))
    return i == l


def pack(m):
    w = m.shape[0]
    h = w // 2
    i, l = iotas((h, w))
    d = l - i
    top, low = m[:h], m[h:]
    rows = jnp.where((d >= 0) & (d < h), top, low)
    rows = jnp.where((d == 0) | (d == h), 0.5 * rows, rows)
    across = jnp.sum(jnp.where(d == h, top, 0.0), axis=0, keepdims=True)
    return rows, jnp.broadcast_to(across, (8, w))


def unpack(p):
    w = p.shape[1]
    h = w // 2
    i, l = iotas((h, w))
    d = l - i
    inside = (d >= 0) & (d < h)
    rows = p[:h]
    across = jnp.broadcast_to(p[h : h + 1], (h, w))
    top = jnp.where(inside, rows, jnp.where(d == h, across, 0.0))
    low = jnp.where(inside, 0.0, rows)
    half = jnp.concatenate([top, low], axis=0).astype(BF16)
    return half + half.T


def side(ref, which, rows=slice(None)):
    return jnp.concatenate([ref[j, rows, :] for j in which], axis=1)


def depth_order(nb):
    return (1, 2, 0, *range(3, nb))


def right_side(nb, w, columns):
    parts = [[ref[j, k * w : (k + 1) * w, :] for ref, j in columns] for k in depth_order(nb)]
    return jnp.concatenate([jnp.concatenate(part, axis=1) for part in parts], axis=0)


def square(nb, w, am, sx):
    for i in range(0, nb, 2):
        pair = range(i, min(i + 2, nb))
        part = mm(side(am, depth_order(nb)), right_side(nb, w, [(am, j) for j in pair]))
        for at, j in enumerate(pair):
            sx[j] = part[:, at * w : (at + 1) * w].astype(BF16)


def square_early(w, am, sx, s00):
    e = slice(0, 3 * w)
    own = side(am, range(3), e)
    part = mm(own, own)
    for j in range(3):
        sx[j, e, :] = part[:, j * w : (j + 1) * w].astype(BF16)
    s00[...] = part[:w, :w]


def square_couplings(nb, w, am, sx, s00, rows, tops):
    def bl(i):
        return slice(i * w, (i + 1) * w)

    total = s00[...]
    for s in range(3, nb):
        total = total + mm(am[s, bl(0), :], am[0, bl(s), :])
        row = mm(am[0, bl(s), :], side(am, range(nb), bl(0)))
        rows[s - 3, :, :w] = row[:, bl(0)]
        rows[s - 3, :, w:] = row[:, bl(s)]
        col = mm(am[0, : 3 * w, :], am[s, bl(0), :])
        tops[s - 3] = col[bl(0), :]
        for r in range(1, nb):
            if r != s:
                sx[r, bl(s), :] = row[:, bl(r)].astype(BF16)
        sx[s, w : 3 * w, :] = col[w:, :].astype(BF16)
    sx[0, bl(0), :] = total.astype(BF16)


def square_diagonals(nb, w, am, sx, rows, tops):
    def bl(i):
        return slice(i * w, (i + 1) * w)

    for s in range(3, nb):
        diag = am[s, bl(s), :]
        row = rows[s - 3] + mm(diag, jnp.concatenate([am[0, bl(s), :], diag], axis=1))
        sx[0, bl(s), :] = row[:, :w].astype(BF16)
        sx[s, bl(s), :] = row[:, w:].astype(BF16)
        sx[s, bl(0), :] = (tops[s - 3] + mm(am[s, bl(0), :], diag)).astype(BF16)


def powers(nb, w, am, sx, fb, v3f, v5f, vb):
    n = nb * w
    at = nb // 2 * w
    halves = (slice(0, at), slice(at, n))

    def bl(i):
        return slice(i * w, (i + 1) * w)

    squares = [jnp.zeros((8, w), F32)]

    def keep_fourth(rows, j, f):
        fb[j, rows, :] = f.astype(BF16)
        squares[0] = squares[0] + jnp.sum((f * f).reshape(-1, 8, w), axis=0)

    right = right_side(nb, w, [(sx, 0), (am, 0)])
    for rows in halves:
        r = mm(side(sx, depth_order(nb), rows), right)
        keep_fourth(rows, 0, r[:, :w])
        v3f[rows, :] = r[:, w:]
        vb[0, rows, :] = r[:, w:].astype(BF16)
    last = nb - 1
    for i in range(1, last, 2):
        pair = [i] if i == last else [i, i + 1]
        right = right_side(nb, w, [(sx, j) for j in pair])
        for rows in halves:
            r = mm(side(sx, depth_order(nb), rows), right)
            for at, j in enumerate(pair):
                keep_fourth(rows, j, r[:, bl(at)])
    right = right_side(nb, w, [(sx, last), (vb, 0)] if nb % 2 == 0 else [(vb, 0)])
    for rows in halves:
        r = mm(side(sx, depth_order(nb), rows), right)
        if nb % 2 == 0:
            keep_fourth(rows, last, r[:, :w])
        v5 = r[:, -w:]
        v5f[rows, :] = v5
        vb[1, rows, :] = v5.astype(BF16)
    return jnp.sum(jnp.sum(squares[0], axis=1, keepdims=True), axis=0, keepdims=True)


def coefficients(total):
    r = lax.rsqrt(lax.rsqrt(lax.rsqrt(total + 1e-06)))
    r2 = r * r
    r3 = r2 * r
    r4 = r2 * r2
    return K1 * r, K3 * r3, K5 * (r4 * r), K7 * (r4 * r3), K9 * (r4 * r4 * r)


def kernel(
    sizes, diag_hbm, x_hbm, y_hbm, lev_hbm, list_hbm, out_ref,
    din, xin, yin, lin, fin, in_sems,
    coup_out, diag_out, diag_out2, rd1, rb1, rd2, rc2, rf3,
    am, v1f, sx, s00, rows, tops, fb, v3f, v5f, vb, cols, rowf,
    send_sems, recv_sems,
):
    nx, ny = sizes
    w = din.shape[0]
    h = w // 2
    merged = ny == 2
    nb = 4 if merged else 5
    ix = lax.axis_index("space")
    iy = lax.axis_index("grp")
    even = lax.rem(ix, 2) == 0
    odd = jnp.logical_not(even)

    def bl(i):
        return slice(i * w, (i + 1) * w)

    def pick(a, b):
        return jnp.where(even, a, b)

    last_x, last_y = ix == nx - 1, iy == ny - 1
    here = [
        jnp.logical_or(odd, jnp.logical_not(last_x)),
        jnp.where(even, ix > 0, jnp.logical_not(last_x)),
    ]
    where_x = [jnp.where(even, ix + 1, ix - 1), jnp.where(even, ix - 1, ix + 1)]
    device = [(jnp.clip(at, 0, nx - 1), iy) for at in where_x]
    upper = [even, odd]
    if merged:
        here.append(jnp.logical_or(iy > 0, jnp.logical_not(last_y)))
        device.append((ix, jnp.where(last_y, iy - 1, iy + 1)))
        upper.append(jnp.logical_not(last_y))
    else:
        here += [iy > 0, jnp.logical_not(last_y)]
        device += [(ix, jnp.maximum(iy - 1, 0)), (ix, jnp.minimum(iy + 1, ny - 1))]
        upper += [iy < 0, iy >= 0]
    peer_role = (0, 1, 2) if merged else (0, 1, 3, 2)
    axis_of = (0, 0, 1) if merged else (0, 0, 1, 1)
    grp_last = jnp.logical_or(even, last_y)
    if merged:
        both = lambda vs: [None, vs[0], jnp.where(grp_last, vs[1], vs[2]), jnp.where(grp_last, vs[2], vs[1])]
    else:
        both = lambda vs: [None, *vs]
    role, peer, axis = both((0, 1, 2, 3)[: nb - 1]), both(peer_role), both(axis_of)
    has, up = both(here), both(upper)
    dev_x, dev_y = both([d[0] for d in device]), both([d[1] for d in device])
    slot_x = pick(1, jnp.where(grp_last, 2, 3) if merged else 2)
    slot_y = jnp.where(grp_last, 3, 2) if merged else 4
    slots = range(1, nb)

    barrier = pltpu.get_barrier_semaphore()
    loads = [
        pltpu.make_async_copy(diag_hbm.at[0, 0], din, in_sems.at[0]),
        pltpu.make_async_copy(lev_hbm.at[0], lin, in_sems.at[3]),
        pltpu.make_async_copy(list_hbm.at[0], fin, in_sems.at[4]),
        pltpu.make_async_copy(y_hbm.at[0, 0], yin, in_sems.at[2]),
        pltpu.make_async_copy(x_hbm.at[0, 0], xin, in_sems.at[1]),
    ]
    for load in loads:
        load.start()
    for s in slots:
        @pl.when(has[s])
        def _():
            pl.semaphore_signal(barrier, inc=1, device_id=(dev_x[s], dev_y[s]), device_id_type=MESH)

    for s in slots:
        @pl.when(jnp.logical_not(has[s]))
        def _():
            rd1[role[s]] = jnp.zeros((h + 8, w), F32)
            rb1[role[s]] = jnp.zeros((w, w), F32)
            rd2[role[s]] = jnp.zeros((h + 8, w), F32)
            rc2[role[s]] = jnp.zeros((w, w), F32)
    for a, last in enumerate((last_x, last_y)):
        @pl.when(last)
        def _():
            rf3[a] = jnp.zeros((w, w), F32)
    for i in slots:
        for j in slots:
            if i != j:
                am[j, bl(i), :] = jnp.zeros((w, w), BF16)
    for load in loads:
        load.wait()
    one_eye = eye(w)
    flag_x = fin[0, 0].astype(F32) * (ix < nx - 1).astype(F32)
    flag_y = fin[0, 1].astype(F32) * (iy < ny - 1).astype(F32)
    raw = din[...]
    onsite = 0.5 * (raw + raw.T) + jnp.where(one_eye, jnp.broadcast_to(lin[...], (w, w)), 0.0)
    diag_out[:h], diag_out[h:] = pack(onsite)
    coup_out[0] = xin[...] * flag_x
    coup_out[1] = yin[...] * flag_y

    count = sum(has[s].astype(jnp.int32) for s in slots)
    pl.semaphore_wait(barrier, count)

    def transfer(src, dst, s, index_send, index_recv):
        return pltpu.make_async_remote_copy(
            src_ref=src, dst_ref=dst, send_sem=send_sems.at[index_send],
            recv_sem=recv_sems.at[index_recv], device_id=(dev_x[s], dev_y[s]), device_id_type=MESH,
        )

    def diag1(s, at):
        return transfer(diag_out, rd1.at[at[s]], s, role[s], at[s])

    def coup1(s, at):
        return transfer(coup_out.at[axis[s]], rb1.at[at[s]], s, 4 + axis[s], 4 + axis[s])

    def diag2(s, at):
        return transfer(diag_out2, rd2.at[at[s]], s, 6 + role[s], 6 + at[s])

    def coup2(s, at):
        return transfer(cols.at[0, s], rc2.at[at[s]], s, 10 + role[s], 10 + at[s])

    def coup3(s, at):
        return transfer(cols.at[1, s], rf3.at[axis[s]], s, 14 + axis[s], 14 + axis[s])

    def sends(make, s):
        if make is coup1:
            return jnp.logical_and(has[s], up[s])
        if make is coup3:
            return jnp.logical_and(has[s], jnp.logical_not(up[s]))
        return has[s]

    def hears(make, s):
        if make is coup1:
            return jnp.logical_and(has[s], jnp.logical_not(up[s]))
        if make is coup3:
            return jnp.logical_and(has[s], up[s])
        return has[s]

    def start(*copies, only=None):
        for make, s in copies:
            there = sends(make, s) if only is None else jnp.logical_and(sends(make, s), only)

            @pl.when(there)
            def _():
                make(s, peer).start()

    def wait_recv(*copies):
        for make, s in copies:
            @pl.when(hears(make, s))
            def _():
                make(s, role).wait_recv()

    late_first = tuple(range(nb - 1, 0, -1))

    def grp_first(*makes):
        if not merged:
            start(*((make, s) for s in late_first[:-1] for make in makes))
            return
        for s, only in ((3, grp_last), (2, jnp.logical_not(grp_last)), (2, grp_last), (3, jnp.logical_not(grp_last))):
            start(*((make, s) for make in makes), only=only)

    grp_first(coup1, diag1)
    start((coup1, 1), (diag1, 1))

    am[0, bl(0), :] = onsite.astype(BF16)
    v1f[bl(0), :] = onsite
    for a, (last, s) in enumerate(((last_x, slot_x), (last_y, slot_y))):
        @pl.when(jnp.logical_not(last))
        def _():
            rb1[pick(0, 1) if a == 0 else nb - 2] = coup_out[a].T

    def hear1(s):
        wait_recv((coup1, s), (diag1, s))
        col = rb1[role[s]]
        half = col.astype(BF16)
        am[s, bl(0), :] = half.T
        am[0, bl(s), :] = half
        v1f[bl(s), :] = col
        am[s, bl(s), :] = unpack(rd1[role[s]])

    for s in slots:
        hear1(s)
    square(nb, w, am, sx)
    total = powers(nb, w, am, sx, fb, v3f, v5f, vb)
    c1, c3, c5, c7, c9 = coefficients(total)

    def finish(step, *blocks):
        for s in blocks:
            for at in ((0, h), (h, w)) if len(blocks) == 1 else ((0, w),):
                r = slice(s * w + at[0], s * w + at[1])
                v79 = mm(side(fb, range(nb), r), side(vb, range(2)))
                low = c1 * v1f[r, :] + c3 * v3f[r, :] + c5 * v5f[r, :]
                cols[step, s, at[0] : at[1], :] = low + c7 * v79[:, :w] + c9 * v79[:, w:]

    tail = tuple(range(nb - 1, 1, -1))
    finish(0, *tail)
    grp_first(coup2)
    finish(0, 0, 1)
    start((coup2, 1))
    c0 = cols[0, 0]
    two = v1f[bl(0), :] + (0.5 * hubbard) * (c0 + c0.T)
    diag_out2[:h], diag_out2[h:] = pack(two)
    grp_first(diag2)
    start((diag2, 1))

    am[0, bl(0), :] = two.astype(BF16)
    v1f[bl(0), :] = two
    for s in slots:
        rowf[s - 1] = (v1f[bl(s), :] + (0.5 * hubbard) * cols[0, s]).T

    def coupling2(s):
        row = rowf[s - 1] + (0.5 * hubbard) * rc2[role[s]]
        half = row.astype(BF16)
        am[s, bl(0), :] = half
        am[0, bl(s), :] = half.T
        v1f[bl(s), :] = row.T

    for s in (1, 2):
        wait_recv((coup2, s), (diag2, s))
        coupling2(s)
        am[s, bl(s), :] = unpack(rd2[role[s]])
    square_early(w, am, sx, s00)
    wait_recv(*((coup2, s) for s in range(3, nb)))
    for s in range(3, nb):
        coupling2(s)
    square_couplings(nb, w, am, sx, s00, rows, tops)
    wait_recv(*((diag2, s) for s in range(3, nb)))
    for s in range(3, nb):
        am[s, bl(s), :] = unpack(rd2[role[s]])
    square_diagonals(nb, w, am, sx, rows, tops)

    total = powers(nb, w, am, sx, fb, v3f, v5f, vb)
    c1, c3, c5, c7, c9 = coefficients(total)
    finish(1, *tail)
    start((coup3, 2), (coup3, 3))
    finish(1, 0, 1)
    start((coup3, 1))
    c0 = cols[1, 0]
    out_ref[0] = 0.5 * (c0 + c0.T) + jnp.where(one_eye, 0.5, 0.0)
    half_x = 0.5 * cols[1, slot_x].T
    half_y = jnp.where(last_y, 0.0, 0.5 * cols[1, slot_y].T)
    wait_recv(*((coup3, s) for s in slots))
    out_ref[1] = half_x + 0.5 * rf3[0]
    out_ref[2] = half_y + 0.5 * rf3[1]
    for make in (diag1, coup1, coup2, diag2, coup3):
        for s in slots:
            @pl.when(sends(make, s))
            def _():
                make(s, peer).wait_send()


def write_out(in_ref, od_ref, ox_ref, oy_ref, sems):
    copies = [
        pltpu.make_async_copy(in_ref.at[i], ref.at[0, 0], sems.at[i])
        for i, ref in enumerate((od_ref, ox_ref, oy_ref))
    ]
    for copy in copies:
        copy.start()
    for copy in copies:
        copy.wait()


def per_device(diag_blocks, x_coupling, y_coupling, levels, listed):
    w = diag_blocks.shape[-1]
    sizes = (lax.axis_size("space"), lax.axis_size("grp"))
    nb = 4 if sizes[1] == 2 else 5
    n = nb * w
    half = w // 2 + 8
    block = jax.ShapeDtypeStruct((1, 1, w, w), F32)
    any_spec = pl.BlockSpec(memory_space=pl.ANY)
    vmem_spec = pl.BlockSpec(memory_space=pltpu.VMEM)
    results = pl.pallas_call(
        functools.partial(kernel, sizes),
        out_shape=pltpu.VMEM((3, w, w), F32),
        in_specs=[any_spec] * 5,
        out_specs=vmem_spec,
        scratch_shapes=[
            pltpu.VMEM((w, w), F32),
            pltpu.VMEM((w, w), F32),
            pltpu.VMEM((w, w), F32),
            pltpu.VMEM((1, w), F32),
            pltpu.SMEM((1, 2), jnp.int32),
            pltpu.SemaphoreType.DMA((5,)),
            pltpu.VMEM((2, w, w), F32),
            pltpu.VMEM((half, w), F32),
            pltpu.VMEM((half, w), F32),
            pltpu.VMEM((nb - 1, half, w), F32),
            pltpu.VMEM((nb - 1, w, w), F32),
            pltpu.VMEM((nb - 1, half, w), F32),
            pltpu.VMEM((nb - 1, w, w), F32),
            pltpu.VMEM((2, w, w), F32),
            pltpu.VMEM((nb, n, w), BF16),
            pltpu.VMEM((n, w), F32),
            pltpu.VMEM((nb, n, w), BF16),
            pltpu.VMEM((w, w), F32),
            pltpu.VMEM((nb - 3, w, 2 * w), F32),
            pltpu.VMEM((nb - 3, w, w), F32),
            pltpu.VMEM((nb, n, w), BF16),
            pltpu.VMEM((n, w), F32),
            pltpu.VMEM((n, w), F32),
            pltpu.VMEM((2, n, w), BF16),
            pltpu.VMEM((2, nb, w, w), F32),
            pltpu.VMEM((nb - 1, w, w), F32),
            pltpu.SemaphoreType.DMA((16,)),
            pltpu.SemaphoreType.DMA((16,)),
        ],
        compiler_params=pltpu.CompilerParams(collective_id=0, has_side_effects=True),
    )(diag_blocks, x_coupling, y_coupling, levels, listed)
    return pl.pallas_call(
        write_out,
        out_shape=(block, block, block),
        in_specs=[vmem_spec],
        out_specs=(any_spec,) * 3,
        scratch_shapes=[pltpu.SemaphoreType.DMA((3,))],
    )(pltpu.with_memory_space_constraint(results, pltpu.VMEM))


def solution(mesh):
    blocks = P("space", "grp", None, None)
    rows = P("space", "grp", None)
    return jax.shard_map(
        per_device,
        mesh=mesh,
        in_specs=(blocks, blocks, blocks, rows, rows),
        out_specs=(blocks, blocks, blocks),
        check_vma=False,
    )
```

```python
import functools

import jax
import jax.numpy as jnp
from jax import lax
from jax.experimental import pallas as pl
from jax.experimental.pallas import tpu as pltpu
from jax.sharding import PartitionSpec as P

hubbard = 1.0
MESH = pl.DeviceIdType.MESH
F32 = jnp.float32
BF16 = jnp.bfloat16
K1, K3, K5, K7, K9 = -1.125, 1.21875, -0.84375, 0.28125, -0.03125


def mm(a, b):
    return jnp.dot(a, b, preferred_element_type=F32)


def iotas(shape):
    return lax.broadcasted_iota(jnp.int32, shape, 0), lax.broadcasted_iota(jnp.int32, shape, 1)


def eye(w):
    i, l = iotas((w, w))
    return i == l


def pack(m):
    w = m.shape[0]
    h = w // 2
    i, l = iotas((h, w))
    d = l - i
    top, low = m[:h], m[h:]
    rows = jnp.where((d >= 0) & (d < h), top, low)
    rows = jnp.where((d == 0) | (d == h), 0.5 * rows, rows)
    across = jnp.sum(jnp.where(d == h, top, 0.0), axis=0, keepdims=True)
    return rows, jnp.broadcast_to(across, (8, w))


def unpack(p):
    w = p.shape[1]
    h = w // 2
    i, l = iotas((h, w))
    d = l - i
    inside = (d >= 0) & (d < h)
    rows = p[:h]
    across = jnp.broadcast_to(p[h : h + 1], (h, w))
    top = jnp.where(inside, rows, jnp.where(d == h, across, 0.0))
    low = jnp.where(inside, 0.0, rows)
    half = jnp.concatenate([top, low], axis=0).astype(BF16)
    return half + half.T


def side(ref, which, rows=slice(None)):
    return jnp.concatenate([ref[j, rows, :] for j in which], axis=1)


def depth_order(nb):
    return (1, 2, 0, *range(3, nb))


def right_side(nb, w, columns):
    parts = [[ref[j, k * w : (k + 1) * w, :] for ref, j in columns] for k in depth_order(nb)]
    return jnp.concatenate([jnp.concatenate(part, axis=1) for part in parts], axis=0)


def square(nb, w, am, sx):
    for i in range(0, nb, 2):
        pair = range(i, min(i + 2, nb))
        part = mm(side(am, depth_order(nb)), right_side(nb, w, [(am, j) for j in pair]))
        for at, j in enumerate(pair):
            sx[j] = part[:, at * w : (at + 1) * w].astype(BF16)


def square_early(w, am, sx, s00):
    e = slice(0, 3 * w)
    own = side(am, range(3), e)
    part = mm(own, own)
    for j in range(3):
        sx[j, e, :] = part[:, j * w : (j + 1) * w].astype(BF16)
    s00[...] = part[:w, :w]


def square_couplings(nb, w, am, sx, s00, rows, tops):
    def bl(i):
        return slice(i * w, (i + 1) * w)

    total = s00[...]
    for s in range(3, nb):
        total = total + mm(am[s, bl(0), :], am[0, bl(s), :])
        row = mm(am[0, bl(s), :], side(am, range(nb), bl(0)))
        rows[s - 3, :, :w] = row[:, bl(0)]
        rows[s - 3, :, w:] = row[:, bl(s)]
        col = mm(am[0, : 3 * w, :], am[s, bl(0), :])
        tops[s - 3] = col[bl(0), :]
        for r in range(1, nb):
            if r != s:
                sx[r, bl(s), :] = row[:, bl(r)].astype(BF16)
        sx[s, w : 3 * w, :] = col[w:, :].astype(BF16)
    sx[0, bl(0), :] = total.astype(BF16)


def square_diagonals(nb, w, am, sx, rows, tops):
    def bl(i):
        return slice(i * w, (i + 1) * w)

    for s in range(3, nb):
        diag = am[s, bl(s), :]
        row = rows[s - 3] + mm(diag, jnp.concatenate([am[0, bl(s), :], diag], axis=1))
        sx[0, bl(s), :] = row[:, :w].astype(BF16)
        sx[s, bl(s), :] = row[:, w:].astype(BF16)
        sx[s, bl(0), :] = (tops[s - 3] + mm(am[s, bl(0), :], diag)).astype(BF16)


def powers(nb, w, am, sx, fb, v3f, v5f, vb):
    n = nb * w
    at = nb // 2 * w
    halves = (slice(0, at), slice(at, n))

    def bl(i):
        return slice(i * w, (i + 1) * w)

    squares = [jnp.zeros((8, w), F32)]

    def keep_fourth(rows, j, f):
        fb[j, rows, :] = f.astype(BF16)
        squares[0] = squares[0] + jnp.sum((f * f).reshape(-1, 8, w), axis=0)

    right = right_side(nb, w, [(sx, 0), (am, 0)])
    for rows in halves:
        r = mm(side(sx, depth_order(nb), rows), right)
        keep_fourth(rows, 0, r[:, :w])
        v3f[rows, :] = r[:, w:]
        vb[0, rows, :] = r[:, w:].astype(BF16)
    last = nb - 1
    for i in range(1, last, 2):
        pair = [i] if i == last else [i, i + 1]
        right = right_side(nb, w, [(sx, j) for j in pair])
        for rows in halves:
            r = mm(side(sx, depth_order(nb), rows), right)
            for at, j in enumerate(pair):
                keep_fourth(rows, j, r[:, bl(at)])
    right = right_side(nb, w, [(sx, last), (vb, 0)] if nb % 2 == 0 else [(vb, 0)])
    for rows in halves:
        r = mm(side(sx, depth_order(nb), rows), right)
        if nb % 2 == 0:
            keep_fourth(rows, last, r[:, :w])
        v5 = r[:, -w:]
        v5f[rows, :] = v5
        vb[1, rows, :] = v5.astype(BF16)
    return jnp.sum(jnp.sum(squares[0], axis=1, keepdims=True), axis=0, keepdims=True)


def coefficients(total):
    r = lax.rsqrt(lax.rsqrt(lax.rsqrt(total + 1e-06)))
    r2 = r * r
    r3 = r2 * r
    r4 = r2 * r2
    return K1 * r, K3 * r3, K5 * (r4 * r), K7 * (r4 * r3), K9 * (r4 * r4 * r)


def kernel(
    sizes, diag_hbm, x_hbm, y_hbm, lev_hbm, list_hbm, out_ref,
    din, xin, yin, lin, fin, in_sems,
    coup_out, diag_out, diag_out2, rd1, rb1, rd2, rc2, rf3,
    am, v1f, sx, s00, rows, tops, fb, v3f, v5f, vb, cols, rowf,
    send_sems, recv_sems,
):
    nx, ny = sizes
    w = din.shape[0]
    h = w // 2
    merged = ny == 2
    nb = 4 if merged else 5
    ix = lax.axis_index("space")
    iy = lax.axis_index("grp")
    even = lax.rem(ix, 2) == 0
    odd = jnp.logical_not(even)

    def bl(i):
        return slice(i * w, (i + 1) * w)

    def pick(a, b):
        return jnp.where(even, a, b)

    last_x, last_y = ix == nx - 1, iy == ny - 1
    here = [
        jnp.logical_or(odd, jnp.logical_not(last_x)),
        jnp.where(even, ix > 0, jnp.logical_not(last_x)),
    ]
    where_x = [jnp.where(even, ix + 1, ix - 1), jnp.where(even, ix - 1, ix + 1)]
    device = [(jnp.clip(at, 0, nx - 1), iy) for at in where_x]
    upper = [even, odd]
    if merged:
        here.append(jnp.logical_or(iy > 0, jnp.logical_not(last_y)))
        device.append((ix, jnp.where(last_y, iy - 1, iy + 1)))
        upper.append(jnp.logical_not(last_y))
    else:
        here += [iy > 0, jnp.logical_not(last_y)]
        device += [(ix, jnp.maximum(iy - 1, 0)), (ix, jnp.minimum(iy + 1, ny - 1))]
        upper += [iy < 0, iy >= 0]
    peer_role = (0, 1, 2) if merged else (0, 1, 3, 2)
    axis_of = (0, 0, 1) if merged else (0, 0, 1, 1)
    grp_last = jnp.logical_or(even, last_y)
    if merged:
        both = lambda vs: [None, vs[0], jnp.where(grp_last, vs[1], vs[2]), jnp.where(grp_last, vs[2], vs[1])]
    else:
        both = lambda vs: [None, *vs]
    role, peer, axis = both((0, 1, 2, 3)[: nb - 1]), both(peer_role), both(axis_of)
    has, up = both(here), both(upper)
    dev_x, dev_y = both([d[0] for d in device]), both([d[1] for d in device])
    slot_x = pick(1, jnp.where(grp_last, 2, 3) if merged else 2)
    slot_y = jnp.where(grp_last, 3, 2) if merged else 4
    slots = range(1, nb)

    barrier = pltpu.get_barrier_semaphore()
    loads = [
        pltpu.make_async_copy(diag_hbm.at[0, 0], din, in_sems.at[0]),
        pltpu.make_async_copy(lev_hbm.at[0], lin, in_sems.at[3]),
        pltpu.make_async_copy(list_hbm.at[0], fin, in_sems.at[4]),
        pltpu.make_async_copy(y_hbm.at[0, 0], yin, in_sems.at[2]),
        pltpu.make_async_copy(x_hbm.at[0, 0], xin, in_sems.at[1]),
    ]
    for load in loads:
        load.start()
    for s in slots:
        @pl.when(has[s])
        def _():
            pl.semaphore_signal(barrier, inc=1, device_id=(dev_x[s], dev_y[s]), device_id_type=MESH)

    for s in slots:
        @pl.when(jnp.logical_not(has[s]))
        def _():
            rd1[role[s]] = jnp.zeros((h + 8, w), F32)
            rb1[role[s]] = jnp.zeros((w, w), F32)
            rd2[role[s]] = jnp.zeros((h + 8, w), F32)
            rc2[role[s]] = jnp.zeros((w, w), F32)
    for a, last in enumerate((last_x, last_y)):
        @pl.when(last)
        def _():
            rf3[a] = jnp.zeros((w, w), F32)
    for i in slots:
        for j in slots:
            if i != j:
                am[j, bl(i), :] = jnp.zeros((w, w), BF16)
    for load in loads:
        load.wait()
    one_eye = eye(w)
    flag_x = fin[0, 0].astype(F32) * (ix < nx - 1).astype(F32)
    flag_y = fin[0, 1].astype(F32) * (iy < ny - 1).astype(F32)
    raw = din[...]
    onsite = 0.5 * (raw + raw.T) + jnp.where(one_eye, jnp.broadcast_to(lin[...], (w, w)), 0.0)
    diag_out[:h], diag_out[h:] = pack(onsite)
    coup_out[0] = xin[...] * flag_x
    coup_out[1] = yin[...] * flag_y

    count = sum(has[s].astype(jnp.int32) for s in slots)
    pl.semaphore_wait(barrier, count)

    def transfer(src, dst, s, index_send, index_recv):
        return pltpu.make_async_remote_copy(
            src_ref=src, dst_ref=dst, send_sem=send_sems.at[index_send],
            recv_sem=recv_sems.at[index_recv], device_id=(dev_x[s], dev_y[s]), device_id_type=MESH,
        )

    def diag1(s, at):
        return transfer(diag_out, rd1.at[at[s]], s, role[s], at[s])

    def coup1(s, at):
        return transfer(coup_out.at[axis[s]], rb1.at[at[s]], s, 4 + axis[s], 4 + axis[s])

    def diag2(s, at):
        return transfer(diag_out2, rd2.at[at[s]], s, 6 + role[s], 6 + at[s])

    def coup2(s, at):
        return transfer(cols.at[0, s], rc2.at[at[s]], s, 10 + role[s], 10 + at[s])

    def coup3(s, at):
        return transfer(cols.at[1, s], rf3.at[axis[s]], s, 14 + axis[s], 14 + axis[s])

    def sends(make, s):
        if make is coup1:
            return jnp.logical_and(has[s], up[s])
        if make is coup3:
            return jnp.logical_and(has[s], jnp.logical_not(up[s]))
        return has[s]

    def hears(make, s):
        if make is coup1:
            return jnp.logical_and(has[s], jnp.logical_not(up[s]))
        if make is coup3:
            return jnp.logical_and(has[s], up[s])
        return has[s]

    def start(*copies, only=None):
        for make, s in copies:
            there = sends(make, s) if only is None else jnp.logical_and(sends(make, s), only)

            @pl.when(there)
            def _():
                make(s, peer).start()

    def wait_recv(*copies):
        for make, s in copies:
            @pl.when(hears(make, s))
            def _():
                make(s, role).wait_recv()

    late_first = tuple(range(nb - 1, 0, -1))

    def grp_first(*makes):
        if not merged:
            start(*((make, s) for s in late_first[:-1] for make in makes))
            return
        for s, only in ((3, grp_last), (2, jnp.logical_not(grp_last)), (2, grp_last), (3, jnp.logical_not(grp_last))):
            start(*((make, s) for make in makes), only=only)

    grp_first(coup1, diag1)
    start((coup1, 1), (diag1, 1))

    am[0, bl(0), :] = onsite.astype(BF16)
    v1f[bl(0), :] = onsite
    for a, (last, s) in enumerate(((last_x, slot_x), (last_y, slot_y))):
        @pl.when(jnp.logical_not(last))
        def _():
            rb1[pick(0, 1) if a == 0 else nb - 2] = coup_out[a].T

    def hear1(s):
        wait_recv((coup1, s), (diag1, s))
        col = rb1[role[s]]
        half = col.astype(BF16)
        am[s, bl(0), :] = half.T
        am[0, bl(s), :] = half
        v1f[bl(s), :] = col
        am[s, bl(s), :] = unpack(rd1[role[s]])

    for s in slots:
        hear1(s)
    square(nb, w, am, sx)
    total = powers(nb, w, am, sx, fb, v3f, v5f, vb)
    c1, c3, c5, c7, c9 = coefficients(total)

    def finish(step, *blocks):
        for s in blocks:
            for at in ((0, h), (h, w)) if len(blocks) == 1 else ((0, w),):
                r = slice(s * w + at[0], s * w + at[1])
                v79 = mm(side(fb, range(nb), r), side(vb, range(2)))
                low = c1 * v1f[r, :] + c3 * v3f[r, :] + c5 * v5f[r, :]
                cols[step, s, at[0] : at[1], :] = low + c7 * v79[:, :w] + c9 * v79[:, w:]

    tail = tuple(range(nb - 1, 1, -1))
    finish(0, *tail)
    grp_first(coup2)
    finish(0, 0, 1)
    start((coup2, 1))
    c0 = cols[0, 0]
    two = v1f[bl(0), :] + (0.5 * hubbard) * (c0 + c0.T)
    diag_out2[:h], diag_out2[h:] = pack(two)
    grp_first(diag2)
    start((diag2, 1))

    am[0, bl(0), :] = two.astype(BF16)
    v1f[bl(0), :] = two
    for s in slots:
        rowf[s - 1] = (v1f[bl(s), :] + (0.5 * hubbard) * cols[0, s]).T

    def coupling2(s):
        row = rowf[s - 1] + (0.5 * hubbard) * rc2[role[s]]
        half = row.astype(BF16)
        am[s, bl(0), :] = half
        am[0, bl(s), :] = half.T
        v1f[bl(s), :] = row.T

    for s in (1, 2):
        wait_recv((coup2, s), (diag2, s))
        coupling2(s)
        am[s, bl(s), :] = unpack(rd2[role[s]])
    square_early(w, am, sx, s00)
    wait_recv(*((coup2, s) for s in range(3, nb)))
    for s in range(3, nb):
        coupling2(s)
    square_couplings(nb, w, am, sx, s00, rows, tops)
    wait_recv(*((diag2, s) for s in range(3, nb)))
    for s in range(3, nb):
        am[s, bl(s), :] = unpack(rd2[role[s]])
    square_diagonals(nb, w, am, sx, rows, tops)

    total = powers(nb, w, am, sx, fb, v3f, v5f, vb)
    c1, c3, c5, c7, c9 = coefficients(total)
    finish(1, *tail)
    start((coup3, 2), (coup3, 3))
    finish(1, 0, 1)
    start((coup3, 1))
    c0 = cols[1, 0]
    out_ref[0] = 0.5 * (c0 + c0.T) + jnp.where(one_eye, 0.5, 0.0)
    half_x = 0.5 * cols[1, slot_x].T
    half_y = jnp.where(last_y, 0.0, 0.5 * cols[1, slot_y].T)
    def wait_send(*makes):
        for make in makes:
            for s in slots:
                @pl.when(sends(make, s))
                def _():
                    make(s, peer).wait_send()

    wait_send(diag1, coup1, coup2, diag2)
    wait_recv(*((coup3, s) for s in slots))
    out_ref[1] = half_x + 0.5 * rf3[0]
    out_ref[2] = half_y + 0.5 * rf3[1]
    wait_send(coup3)


def write_out(in_ref, od_ref, ox_ref, oy_ref, sems):
    copies = [
        pltpu.make_async_copy(in_ref.at[i], ref.at[0, 0], sems.at[i])
        for i, ref in enumerate((od_ref, ox_ref, oy_ref))
    ]
    for copy in copies:
        copy.start()
    for copy in copies:
        copy.wait()


def per_device(diag_blocks, x_coupling, y_coupling, levels, listed):
    w = diag_blocks.shape[-1]
    sizes = (lax.axis_size("space"), lax.axis_size("grp"))
    nb = 4 if sizes[1] == 2 else 5
    n = nb * w
    half = w // 2 + 8
    block = jax.ShapeDtypeStruct((1, 1, w, w), F32)
    any_spec = pl.BlockSpec(memory_space=pl.ANY)
    vmem_spec = pl.BlockSpec(memory_space=pltpu.VMEM)
    results = pl.pallas_call(
        functools.partial(kernel, sizes),
        out_shape=pltpu.VMEM((3, w, w), F32),
        in_specs=[any_spec] * 5,
        out_specs=vmem_spec,
        scratch_shapes=[
            pltpu.VMEM((w, w), F32),
            pltpu.VMEM((w, w), F32),
            pltpu.VMEM((w, w), F32),
            pltpu.VMEM((1, w), F32),
            pltpu.SMEM((1, 2), jnp.int32),
            pltpu.SemaphoreType.DMA((5,)),
            pltpu.VMEM((2, w, w), F32),
            pltpu.VMEM((half, w), F32),
            pltpu.VMEM((half, w), F32),
            pltpu.VMEM((nb - 1, half, w), F32),
            pltpu.VMEM((nb - 1, w, w), F32),
            pltpu.VMEM((nb - 1, half, w), F32),
            pltpu.VMEM((nb - 1, w, w), F32),
            pltpu.VMEM((2, w, w), F32),
            pltpu.VMEM((nb, n, w), BF16),
            pltpu.VMEM((n, w), F32),
            pltpu.VMEM((nb, n, w), BF16),
            pltpu.VMEM((w, w), F32),
            pltpu.VMEM((nb - 3, w, 2 * w), F32),
            pltpu.VMEM((nb - 3, w, w), F32),
            pltpu.VMEM((nb, n, w), BF16),
            pltpu.VMEM((n, w), F32),
            pltpu.VMEM((n, w), F32),
            pltpu.VMEM((2, n, w), BF16),
            pltpu.VMEM((2, nb, w, w), F32),
            pltpu.VMEM((nb - 1, w, w), F32),
            pltpu.SemaphoreType.DMA((16,)),
            pltpu.SemaphoreType.DMA((16,)),
        ],
        compiler_params=pltpu.CompilerParams(collective_id=0, has_side_effects=True),
    )(diag_blocks, x_coupling, y_coupling, levels, listed)
    return pl.pallas_call(
        write_out,
        out_shape=(block, block, block),
        in_specs=[vmem_spec],
        out_specs=(any_spec,) * 3,
        scratch_shapes=[pltpu.SemaphoreType.DMA((3,))],
    )(pltpu.with_memory_space_constraint(results, pltpu.VMEM))


def solution(mesh):
    blocks = P("space", "grp", None, None)
    rows = P("space", "grp", None)
    return jax.shard_map(
        per_device,
        mesh=mesh,
        in_specs=(blocks, blocks, blocks, rows, rows),
        out_specs=(blocks, blocks, blocks),
        check_vma=False,
    )
```

```python
import functools

import jax
import jax.numpy as jnp
from jax import lax
from jax.experimental import pallas as pl
from jax.experimental.pallas import tpu as pltpu
from jax.sharding import PartitionSpec as P

hubbard = 1.0
MESH = pl.DeviceIdType.MESH
F32 = jnp.float32
BF16 = jnp.bfloat16
K1, K3, K5, K7, K9 = -1.125, 1.21875, -0.84375, 0.28125, -0.03125


def mm(a, b):
    return jnp.dot(a, b, preferred_element_type=F32)


def iotas(shape):
    return lax.broadcasted_iota(jnp.int32, shape, 0), lax.broadcasted_iota(jnp.int32, shape, 1)


def eye(w):
    i, l = iotas((w, w))
    return i == l


def pack(m):
    w = m.shape[0]
    h = w // 2
    i, l = iotas((h, w))
    d = l - i
    top, low = m[:h], m[h:]
    rows = jnp.where((d >= 0) & (d < h), top, low)
    rows = jnp.where((d == 0) | (d == h), 0.5 * rows, rows)
    across = jnp.sum(jnp.where(d == h, top, 0.0), axis=0, keepdims=True)
    return rows, jnp.broadcast_to(across, (8, w))


def unpack(p):
    w = p.shape[1]
    h = w // 2
    i, l = iotas((h, w))
    d = l - i
    inside = (d >= 0) & (d < h)
    rows = p[:h]
    across = jnp.broadcast_to(p[h : h + 1], (h, w))
    top = jnp.where(inside, rows, jnp.where(d == h, across, 0.0))
    low = jnp.where(inside, 0.0, rows)
    half = jnp.concatenate([top, low], axis=0).astype(BF16)
    return half + half.T


def side(ref, which, rows=slice(None)):
    return jnp.concatenate([ref[j, rows, :] for j in which], axis=1)


def depth_order(nb):
    return (1, 2, 0, *range(3, nb))


def right_side(nb, w, columns):
    parts = [[ref[j, k * w : (k + 1) * w, :] for ref, j in columns] for k in depth_order(nb)]
    return jnp.concatenate([jnp.concatenate(part, axis=1) for part in parts], axis=0)


def square(nb, w, am, sx):
    for i in range(0, nb, 2):
        pair = range(i, min(i + 2, nb))
        part = mm(side(am, depth_order(nb)), right_side(nb, w, [(am, j) for j in pair]))
        for at, j in enumerate(pair):
            sx[j] = part[:, at * w : (at + 1) * w].astype(BF16)


def square_early(w, am, sx, s00):
    e = slice(0, 3 * w)
    own = side(am, range(3), e)
    part = mm(own, own)
    for j in range(3):
        sx[j, e, :] = part[:, j * w : (j + 1) * w].astype(BF16)
    s00[...] = part[:w, :w]


def square_couplings(nb, w, am, sx, s00, rows, tops):
    def bl(i):
        return slice(i * w, (i + 1) * w)

    total = s00[...]
    for s in range(3, nb):
        total = total + mm(am[s, bl(0), :], am[0, bl(s), :])
        row = mm(am[0, bl(s), :], side(am, range(nb), bl(0)))
        rows[s - 3, :, :w] = row[:, bl(0)]
        rows[s - 3, :, w:] = row[:, bl(s)]
        col = mm(am[0, : 3 * w, :], am[s, bl(0), :])
        tops[s - 3] = col[bl(0), :]
        for r in range(1, nb):
            if r != s:
                sx[r, bl(s), :] = row[:, bl(r)].astype(BF16)
        sx[s, w : 3 * w, :] = col[w:, :].astype(BF16)
    sx[0, bl(0), :] = total.astype(BF16)


def square_diagonals(nb, w, am, sx, rows, tops):
    def bl(i):
        return slice(i * w, (i + 1) * w)

    for s in range(3, nb):
        diag = am[s, bl(s), :]
        row = rows[s - 3] + mm(diag, jnp.concatenate([am[0, bl(s), :], diag], axis=1))
        sx[0, bl(s), :] = row[:, :w].astype(BF16)
        sx[s, bl(s), :] = row[:, w:].astype(BF16)
        sx[s, bl(0), :] = (tops[s - 3] + mm(am[s, bl(0), :], diag)).astype(BF16)


def powers(nb, w, am, sx, fb, v3f, v5f, vb):
    n = nb * w
    at = nb // 2 * w
    halves = (slice(0, at), slice(at, n))

    def bl(i):
        return slice(i * w, (i + 1) * w)

    squares = [jnp.zeros((8, w), F32)]

    def keep_fourth(rows, j, f):
        fb[j, rows, :] = f.astype(BF16)
        squares[0] = squares[0] + jnp.sum((f * f).reshape(-1, 8, w), axis=0)

    right = right_side(nb, w, [(sx, 0), (am, 0)])
    for rows in halves:
        r = mm(side(sx, depth_order(nb), rows), right)
        keep_fourth(rows, 0, r[:, :w])
        v3f[rows, :] = r[:, w:]
        vb[0, rows, :] = r[:, w:].astype(BF16)
    last = nb - 1
    for i in range(1, last, 2):
        pair = [i] if i == last else [i, i + 1]
        right = right_side(nb, w, [(sx, j) for j in pair])
        for rows in halves:
            r = mm(side(sx, depth_order(nb), rows), right)
            for at, j in enumerate(pair):
                keep_fourth(rows, j, r[:, bl(at)])
    right = right_side(nb, w, [(sx, last), (vb, 0)] if nb % 2 == 0 else [(vb, 0)])
    for rows in halves:
        r = mm(side(sx, depth_order(nb), rows), right)
        if nb % 2 == 0:
            keep_fourth(rows, last, r[:, :w])
        v5 = r[:, -w:]
        v5f[rows, :] = v5
        vb[1, rows, :] = v5.astype(BF16)
    return jnp.sum(jnp.sum(squares[0], axis=1, keepdims=True), axis=0, keepdims=True)


def coefficients(total):
    r = lax.rsqrt(lax.rsqrt(lax.rsqrt(total + 1e-06)))
    r2 = r * r
    r3 = r2 * r
    r4 = r2 * r2
    return K1 * r, K3 * r3, K5 * (r4 * r), K7 * (r4 * r3), K9 * (r4 * r4 * r)


def kernel(
    sizes, diag_hbm, x_hbm, y_hbm, lev_hbm, list_hbm, out_ref,
    din, xin, yin, lin, fin, in_sems,
    coup_out, diag_out, diag_out2, rd1, rb1, rd2, rc2, rf3,
    am, v1f, sx, s00, rows, tops, fb, v3f, v5f, vb, cols, rowf,
    send_sems, recv_sems,
):
    nx, ny = sizes
    w = din.shape[0]
    h = w // 2
    merged = ny == 2
    nb = 4 if merged else 5
    ix = lax.axis_index("space")
    iy = lax.axis_index("grp")
    even = lax.rem(ix, 2) == 0
    odd = jnp.logical_not(even)

    def bl(i):
        return slice(i * w, (i + 1) * w)

    def pick(a, b):
        return jnp.where(even, a, b)

    last_x, last_y = ix == nx - 1, iy == ny - 1
    here = [
        jnp.logical_or(odd, jnp.logical_not(last_x)),
        jnp.where(even, ix > 0, jnp.logical_not(last_x)),
    ]
    where_x = [jnp.where(even, ix + 1, ix - 1), jnp.where(even, ix - 1, ix + 1)]
    device = [(jnp.clip(at, 0, nx - 1), iy) for at in where_x]
    upper = [even, odd]
    if merged:
        here.append(jnp.logical_or(iy > 0, jnp.logical_not(last_y)))
        device.append((ix, jnp.where(last_y, iy - 1, iy + 1)))
        upper.append(jnp.logical_not(last_y))
    else:
        here += [iy > 0, jnp.logical_not(last_y)]
        device += [(ix, jnp.maximum(iy - 1, 0)), (ix, jnp.minimum(iy + 1, ny - 1))]
        upper += [iy < 0, iy >= 0]
    peer_role = (0, 1, 2) if merged else (0, 1, 3, 2)
    axis_of = (0, 0, 1) if merged else (0, 0, 1, 1)
    grp_last = jnp.logical_or(even, last_y)
    if merged:
        both = lambda vs: [None, vs[0], jnp.where(grp_last, vs[1], vs[2]), jnp.where(grp_last, vs[2], vs[1])]
    else:
        both = lambda vs: [None, *vs]
    role, peer, axis = both((0, 1, 2, 3)[: nb - 1]), both(peer_role), both(axis_of)
    has, up = both(here), both(upper)
    dev_x, dev_y = both([d[0] for d in device]), both([d[1] for d in device])
    slot_x = pick(1, jnp.where(grp_last, 2, 3) if merged else 2)
    slot_y = jnp.where(grp_last, 3, 2) if merged else 4
    slots = range(1, nb)

    barrier = pltpu.get_barrier_semaphore()
    loads = [
        pltpu.make_async_copy(diag_hbm.at[0, 0], din, in_sems.at[0]),
        pltpu.make_async_copy(lev_hbm.at[0], lin, in_sems.at[3]),
        pltpu.make_async_copy(list_hbm.at[0], fin, in_sems.at[4]),
        pltpu.make_async_copy(y_hbm.at[0, 0], yin, in_sems.at[2]),
        pltpu.make_async_copy(x_hbm.at[0, 0], xin, in_sems.at[1]),
    ]
    for load in loads:
        load.start()
    for s in reversed(slots):
        @pl.when(has[s])
        def _():
            pl.semaphore_signal(barrier, inc=1, device_id=(dev_x[s], dev_y[s]), device_id_type=MESH)

    for s in slots:
        @pl.when(jnp.logical_not(has[s]))
        def _():
            rd1[role[s]] = jnp.zeros((h + 8, w), F32)
            rb1[role[s]] = jnp.zeros((w, w), F32)
            rd2[role[s]] = jnp.zeros((h + 8, w), F32)
            rc2[role[s]] = jnp.zeros((w, w), F32)
    for a, last in enumerate((last_x, last_y)):
        @pl.when(last)
        def _():
            rf3[a] = jnp.zeros((w, w), F32)
    for i in slots:
        for j in slots:
            if i != j:
                am[j, bl(i), :] = jnp.zeros((w, w), BF16)
    for load in loads:
        load.wait()
    one_eye = eye(w)
    flag_x = fin[0, 0].astype(F32) * (ix < nx - 1).astype(F32)
    flag_y = fin[0, 1].astype(F32) * (iy < ny - 1).astype(F32)
    raw = din[...]
    onsite = 0.5 * (raw + raw.T) + jnp.where(one_eye, jnp.broadcast_to(lin[...], (w, w)), 0.0)
    diag_out[:h], diag_out[h:] = pack(onsite)
    coup_out[0] = xin[...] * flag_x
    coup_out[1] = yin[...] * flag_y

    count = sum(has[s].astype(jnp.int32) for s in slots)
    pl.semaphore_wait(barrier, count)

    def transfer(src, dst, s, index_send, index_recv):
        return pltpu.make_async_remote_copy(
            src_ref=src, dst_ref=dst, send_sem=send_sems.at[index_send],
            recv_sem=recv_sems.at[index_recv], device_id=(dev_x[s], dev_y[s]), device_id_type=MESH,
        )

    def diag1(s, at):
        return transfer(diag_out, rd1.at[at[s]], s, role[s], at[s])

    def coup1(s, at):
        return transfer(coup_out.at[axis[s]], rb1.at[at[s]], s, 4 + axis[s], 4 + axis[s])

    def diag2(s, at):
        return transfer(diag_out2, rd2.at[at[s]], s, 6 + role[s], 6 + at[s])

    def coup2(s, at):
        return transfer(cols.at[0, s], rc2.at[at[s]], s, 10 + role[s], 10 + at[s])

    def coup3(s, at):
        return transfer(cols.at[1, s], rf3.at[axis[s]], s, 14 + axis[s], 14 + axis[s])

    def sends(make, s):
        if make is coup1:
            return jnp.logical_and(has[s], up[s])
        if make is coup3:
            return jnp.logical_and(has[s], jnp.logical_not(up[s]))
        return has[s]

    def hears(make, s):
        if make is coup1:
            return jnp.logical_and(has[s], jnp.logical_not(up[s]))
        if make is coup3:
            return jnp.logical_and(has[s], up[s])
        return has[s]

    def start(*copies, only=None):
        for make, s in copies:
            there = sends(make, s) if only is None else jnp.logical_and(sends(make, s), only)

            @pl.when(there)
            def _():
                make(s, peer).start()

    def wait_recv(*copies):
        for make, s in copies:
            @pl.when(hears(make, s))
            def _():
                make(s, role).wait_recv()

    late_first = tuple(range(nb - 1, 0, -1))

    def grp_first(*makes):
        if not merged:
            start(*((make, s) for s in late_first[:-1] for make in makes))
            return
        for s, only in ((3, grp_last), (2, jnp.logical_not(grp_last)), (2, grp_last), (3, jnp.logical_not(grp_last))):
            start(*((make, s) for make in makes), only=only)

    grp_first(coup1, diag1)
    start((coup1, 1), (diag1, 1))

    am[0, bl(0), :] = onsite.astype(BF16)
    v1f[bl(0), :] = onsite
    for a, (last, s) in enumerate(((last_x, slot_x), (last_y, slot_y))):
        @pl.when(jnp.logical_not(last))
        def _():
            rb1[pick(0, 1) if a == 0 else nb - 2] = coup_out[a].T

    def hear1(s):
        wait_recv((coup1, s), (diag1, s))
        col = rb1[role[s]]
        half = col.astype(BF16)
        am[s, bl(0), :] = half.T
        am[0, bl(s), :] = half
        v1f[bl(s), :] = col
        am[s, bl(s), :] = unpack(rd1[role[s]])

    for s in slots:
        hear1(s)
    square(nb, w, am, sx)
    total = powers(nb, w, am, sx, fb, v3f, v5f, vb)
    c1, c3, c5, c7, c9 = coefficients(total)

    def finish(step, *blocks):
        for s in blocks:
            for at in ((0, h), (h, w)) if len(blocks) == 1 else ((0, w),):
                r = slice(s * w + at[0], s * w + at[1])
                v79 = mm(side(fb, range(nb), r), side(vb, range(2)))
                low = c1 * v1f[r, :] + c3 * v3f[r, :] + c5 * v5f[r, :]
                cols[step, s, at[0] : at[1], :] = low + c7 * v79[:, :w] + c9 * v79[:, w:]

    tail = tuple(range(nb - 1, 1, -1))
    finish(0, *tail)
    grp_first(coup2)
    finish(0, 0, 1)
    start((coup2, 1))
    c0 = cols[0, 0]
    two = v1f[bl(0), :] + (0.5 * hubbard) * (c0 + c0.T)
    diag_out2[:h], diag_out2[h:] = pack(two)
    grp_first(diag2)
    start((diag2, 1))

    am[0, bl(0), :] = two.astype(BF16)
    v1f[bl(0), :] = two
    for s in slots:
        rowf[s - 1] = (v1f[bl(s), :] + (0.5 * hubbard) * cols[0, s]).T

    def coupling2(s):
        row = rowf[s - 1] + (0.5 * hubbard) * rc2[role[s]]
        half = row.astype(BF16)
        am[s, bl(0), :] = half
        am[0, bl(s), :] = half.T
        v1f[bl(s), :] = row.T

    for s in (1, 2):
        wait_recv((coup2, s), (diag2, s))
        coupling2(s)
        am[s, bl(s), :] = unpack(rd2[role[s]])
    square_early(w, am, sx, s00)
    wait_recv(*((coup2, s) for s in range(3, nb)))
    for s in range(3, nb):
        coupling2(s)
    square_couplings(nb, w, am, sx, s00, rows, tops)
    wait_recv(*((diag2, s) for s in range(3, nb)))
    for s in range(3, nb):
        am[s, bl(s), :] = unpack(rd2[role[s]])
    square_diagonals(nb, w, am, sx, rows, tops)

    total = powers(nb, w, am, sx, fb, v3f, v5f, vb)
    c1, c3, c5, c7, c9 = coefficients(total)
    finish(1, *tail)
    start((coup3, 2), (coup3, 3))
    finish(1, 0, 1)
    start((coup3, 1))
    c0 = cols[1, 0]
    out_ref[0] = 0.5 * (c0 + c0.T) + jnp.where(one_eye, 0.5, 0.0)
    half_x = 0.5 * cols[1, slot_x].T
    half_y = jnp.where(last_y, 0.0, 0.5 * cols[1, slot_y].T)
    def wait_send(*makes):
        for make in makes:
            for s in slots:
                @pl.when(sends(make, s))
                def _():
                    make(s, peer).wait_send()

    wait_send(diag1, coup1, coup2, diag2)
    wait_recv(*((coup3, s) for s in slots))
    out_ref[1] = half_x + 0.5 * rf3[0]
    out_ref[2] = half_y + 0.5 * rf3[1]
    wait_send(coup3)


def write_out(in_ref, od_ref, ox_ref, oy_ref, sems):
    copies = [
        pltpu.make_async_copy(in_ref.at[i], ref.at[0, 0], sems.at[i])
        for i, ref in enumerate((od_ref, ox_ref, oy_ref))
    ]
    for copy in copies:
        copy.start()
    for copy in copies:
        copy.wait()


def per_device(diag_blocks, x_coupling, y_coupling, levels, listed):
    w = diag_blocks.shape[-1]
    sizes = (lax.axis_size("space"), lax.axis_size("grp"))
    nb = 4 if sizes[1] == 2 else 5
    n = nb * w
    half = w // 2 + 8
    block = jax.ShapeDtypeStruct((1, 1, w, w), F32)
    any_spec = pl.BlockSpec(memory_space=pl.ANY)
    vmem_spec = pl.BlockSpec(memory_space=pltpu.VMEM)
    results = pl.pallas_call(
        functools.partial(kernel, sizes),
        out_shape=pltpu.VMEM((3, w, w), F32),
        in_specs=[any_spec] * 5,
        out_specs=vmem_spec,
        scratch_shapes=[
            pltpu.VMEM((w, w), F32),
            pltpu.VMEM((w, w), F32),
            pltpu.VMEM((w, w), F32),
            pltpu.VMEM((1, w), F32),
            pltpu.SMEM((1, 2), jnp.int32),
            pltpu.SemaphoreType.DMA((5,)),
            pltpu.VMEM((2, w, w), F32),
            pltpu.VMEM((half, w), F32),
            pltpu.VMEM((half, w), F32),
            pltpu.VMEM((nb - 1, half, w), F32),
            pltpu.VMEM((nb - 1, w, w), F32),
            pltpu.VMEM((nb - 1, half, w), F32),
            pltpu.VMEM((nb - 1, w, w), F32),
            pltpu.VMEM((2, w, w), F32),
            pltpu.VMEM((nb, n, w), BF16),
            pltpu.VMEM((n, w), F32),
            pltpu.VMEM((nb, n, w), BF16),
            pltpu.VMEM((w, w), F32),
            pltpu.VMEM((nb - 3, w, 2 * w), F32),
            pltpu.VMEM((nb - 3, w, w), F32),
            pltpu.VMEM((nb, n, w), BF16),
            pltpu.VMEM((n, w), F32),
            pltpu.VMEM((n, w), F32),
            pltpu.VMEM((2, n, w), BF16),
            pltpu.VMEM((2, nb, w, w), F32),
            pltpu.VMEM((nb - 1, w, w), F32),
            pltpu.SemaphoreType.DMA((16,)),
            pltpu.SemaphoreType.DMA((16,)),
        ],
        compiler_params=pltpu.CompilerParams(collective_id=0, has_side_effects=True),
    )(diag_blocks, x_coupling, y_coupling, levels, listed)
    return pl.pallas_call(
        write_out,
        out_shape=(block, block, block),
        in_specs=[vmem_spec],
        out_specs=(any_spec,) * 3,
        scratch_shapes=[pltpu.SemaphoreType.DMA((3,))],
    )(pltpu.with_memory_space_constraint(results, pltpu.VMEM))


def solution(mesh):
    blocks = P("space", "grp", None, None)
    rows = P("space", "grp", None)
    return jax.shard_map(
        per_device,
        mesh=mesh,
        in_specs=(blocks, blocks, blocks, rows, rows),
        out_specs=(blocks, blocks, blocks),
        check_vma=False,
    )
```
